512 devices in a mesh: wide: 128 (over y, z, core), pair: 4 (over x).
Axes of the slice: x: 4, y: 8, z: 8, core: 2. Of those that a mesh axis runs over, the one named last changes fastest.
Arguments:
- blocks: bfloat16 [2048, 1024, 512], P('pair', 'wide'), may hold values from -6 to 6
- basis_a: bfloat16 [1024, 64], replicated, may hold values from -0.1875 to 0.1875
- basis_b: bfloat16 [512, 64], replicated, may hold values from -0.25 to 0.25
- sketch: bfloat16 [2048, 64], P(('pair', 'wide')), may hold values from -6 to 6
Outputs:
- transfer: float32 [4096, 64], P(('wide', 'pair'))
- coefficients: float32 [2048, 64], P(('pair', 'wide'))
The draws below stay inside these ranges and needn't reach their ends.
All inputs are finite; a program needn't handle non-finite values.
Results may differ from the reference program's by a relative error of at most 0.0041.
Values may be sent and summed in bfloat16 or wider, within the bound.
A program may use at most 64 MiB of HBM per device.

```python
import jax
import jax.numpy as jnp
from jax import lax

CA = 1024
CB = 512
RA = 64
RB = 64
K = 64
F = 2048


def steps_of(stream_key, extent, pieces, low, top_value):
    loudness = 1.0
    for position, parts in pieces:
        steps = jax.random.uniform(jax.random.fold_in(jax.random.fold_in(stream_key, 6), position), (parts,), jnp.float32, low / len(pieces), top_value / len(pieces))
        loudness = loudness * jnp.repeat(jnp.exp(steps), extent[position] // parts).reshape((-1,) + (1,) * (len(extent) - 1 - position))
    return loudness


def normal_values(stream_key, extent, scale, most, cuts=(), held_as=jnp.bfloat16):
    factor_of = steps_of(stream_key, extent, cuts, -0.22, 0.18) if cuts else 1.0
    values = jax.random.normal(stream_key, extent, jnp.float32) * scale * factor_of
    return jnp.minimum(jnp.maximum(values, -most), most).astype(held_as)


def setup_inputs(seed: int = 0) -> dict:
    streams_of = jax.random.split(jax.random.key(seed), 5)
    blocks = normal_values(streams_of[0], (F, CA, CB), 1.0, 6.0, ((0, 4), (1, 128)))
    basis_a = normal_values(streams_of[1], (CA, RA), CA ** -0.5, 0.1875)
    basis_b = normal_values(streams_of[2], (CB, RB), CB ** -0.5, 0.25)
    sketch = normal_values(streams_of[3], (F, K), 1.0, 6.0, ((0, 512),))
    return {"blocks": blocks, "basis_a": basis_a, "basis_b": basis_b, "sketch": sketch}


def reference(blocks, basis_a, basis_b, sketch):

    def per_fibre(fibre_block):
        narrowed = jnp.dot(fibre_block.astype(jnp.float32), basis_b.astype(jnp.float32), preferred_element_type=jnp.float32).astype(jnp.bfloat16)
        folded = jnp.dot(basis_a.T.astype(jnp.float32), narrowed.astype(jnp.float32), preferred_element_type=jnp.float32).astype(jnp.bfloat16)
        return folded.reshape(RA * RB)
    projected = lax.map(per_fibre, blocks)
    sketched = jnp.dot(projected.T.astype(jnp.float32), sketch.astype(jnp.float32), preferred_element_type=jnp.float32)
    gram = jnp.dot(sketched.T, sketched, precision=lax.Precision.HIGHEST)
    lower = jnp.linalg.cholesky(gram)
    parent = lax.linalg.triangular_solve(lower, sketched, left_side=False, lower=True, transpose_a=True)
    transfer = parent * jnp.sqrt(jnp.float32(RA * RB))
    coefficients = jnp.dot(projected.astype(jnp.float32), parent, precision=lax.Precision.HIGHEST)
    return (transfer, coefficients)
```

```python
import functools

import jax
import jax.numpy as jnp
from jax import lax
from jax.experimental import pallas as pl
from jax.experimental.pallas import tpu as pltpu
from jax.sharding import PartitionSpec as P

MESH = pl.DeviceIdType.MESH
F32 = jnp.float32
BF16 = jnp.bfloat16
CONTRACT_LAST = (((1,), (1,)), ((), ()))
CONTRACT_FIRST = (((0,), (0,)), ((), ()))


def iota(shape, dim):
    return lax.broadcasted_iota(jnp.int32, shape, dim)


def dot(a, b, dims=(((1,), (0,)), ((), ())), precision=None):
    return lax.dot_general(a, b, dims, preferred_element_type=F32, precision=precision)


def low_half(shape):
    return iota(shape, 1) < 64


def swap_halves(v):
    return pltpu.roll(v, 64, 1)


def one_hot(mask):
    return jnp.where(mask, 1.0, 0.0).astype(BF16)


def kernel(sizes, blocks, basis_bt, basis_at, sketch, transfer, coefficients, *scratch):
    X, Y, Z = sizes
    ZC = Z * 2
    YL = max(Y // 2, 1)
    chips = Y * Z
    FX = chips * 8
    FC = FX // 8
    (block_in, wide_n, packed, packed_in, s_own, s_zc, s_y, s_all, t_out, t_in, sp_out, sp_in, z_out, z_in,
     mz, s_full, m_to, m_from, w_rows, gram_out, gram_in, y_out, y_in, y2_out, y2_in, x_mat,
     in_sem, s_a, r_a, s_b, r_b, s_p, r_p, s_t, r_t, s_z1, r_z1, s_y1, r_y1, s_z2, r_z2, s_x1, r_x1,
     s_g, r_g, s_yz, r_yz, s_yy, r_yy) = scratch

    wide = lax.axis_index("wide")
    x = lax.axis_index("pair")
    core = wide % 2
    chip = wide // 2
    z = chip % Z
    y = chip // Z

    def at(dx=0, dy=0, dz=0, dc=0):
        row = ((y + dy) % Y) * Z + (z + dz) % Z
        return (row * 2 + (core + dc) % 2, (x + dx) % X)

    waits = []

    def send(src, dst, ssem, rsem, peer):
        copy = pltpu.make_async_remote_copy(
            src_ref=src, dst_ref=dst, send_sem=ssem, recv_sem=rsem, device_id=peer, device_id_type=MESH
        )
        copy.start()
        waits.append(copy)
        return copy

    def receive(copies):
        for copy in copies:
            copy.wait_recv()

    zc_peers = [(dc, dz) for dc in range(2) for dz in range(Z) if dc or dz]
    yc_peers = [(dc, dy) for dc in range(2) for dy in range(Y) if dc or dy]
    xc_peers = [(dc, dx) for dc in range(2) for dx in range(X) if dc or dx]

    loads = [
        pltpu.make_async_copy(blocks.at[pl.ds(i * FX, FX)], block_in.at[i], in_sem.at[i]) for i in range(8)
    ]
    for load in loads:
        load.start()

    barrier = pltpu.get_barrier_semaphore()
    met = 0
    for dc, dz in zc_peers:
        pl.semaphore_signal(barrier, inc=1, device_id=at(dz=dz, dc=dc), device_id_type=MESH)
        met += 1
    for dc, dy in yc_peers:
        if dy:
            pl.semaphore_signal(barrier, inc=1, device_id=at(dy=dy, dc=dc), device_id_type=MESH)
            met += 1
    for dc, dx in xc_peers:
        if dx:
            pl.semaphore_signal(barrier, inc=1, device_id=at(dx=dx, dc=dc), device_id_type=MESH)
            met += 1

    twice = one_hot(iota((64, 128), 1) % 64 == iota((64, 128), 0))
    s_mine = dot(sketch[...], twice)
    s_own[...] = s_mine
    zc = z * 2 + core
    s_zc[zc] = s_mine
    pl.semaphore_wait(barrier, met)

    got_a = [
        send(s_own, s_zc.at[zc], s_a.at[dc, dz], r_a.at[dc, dz], at(dz=dz, dc=dc)) for dc, dz in zc_peers
    ]

    basis2 = jnp.concatenate([basis_bt[...], basis_bt[...]], axis=0)

    def narrow(i, carry):
        pltpu.make_async_copy(blocks.at[pl.ds(i * FX, FX)], block_in.at[i], in_sem.at[i]).wait()
        wide_n[...] = dot(block_in[i], basis2, CONTRACT_LAST)
        rows = pl.ds(pl.multiple_of(i * FC, FC), FC)
        low = low_half((FC, 128))
        odd = (iota((FC, 128), 1) // 32) % 2 == 1
        for t in range(2):
            part = [wide_n[pl.ds(t * 4 + q, FC, stride=8), :] for q in range(4)]
            first = jnp.where(low, part[0], part[2])
            second = jnp.where(low, part[1], part[3])
            lanes = slice(t * 128, t * 128 + 128)
            packed[0, rows, lanes] = jnp.where(odd, pltpu.roll(second, 32, 1), first).astype(BF16)
            packed[1, rows, lanes] = jnp.where(odd, second, pltpu.roll(first, 96, 1)).astype(BF16)
        return carry

    lax.fori_loop(0, 4, narrow, 0)

    receive(got_a)
    half = ZC // 2
    lo = jnp.concatenate([s_zc[i] for i in range(half)], axis=0)
    hi = jnp.concatenate([s_zc[half + i] for i in range(half)], axis=0)
    rows_h = half * 4
    s_y[y] = jnp.where(low_half((rows_h, 128)), lo, hi).astype(BF16)
    got_b = [send(s_y.at[y], s_y.at[y], s_b.at[dy], r_b.at[dy], at(dy=dy)) for dy in range(1, Y)]

    lax.fori_loop(4, 8, narrow, 0)
    partner = at(dc=1)
    got_p = send(packed.at[1 - core], packed_in, s_p, r_p, partner)

    AB = min(chips * 16, 128)
    base = pl.multiple_of((chip * 16 // AB) * AB, AB)
    a_part = basis_at[:, pl.ds(base, AB)]
    MR = chips * 4

    def chip_of(index):
        zy = index // 4
        return (zy % Y) * Z + zy // Y

    col = iota((AB, 256), 1)
    pick = base + iota((AB, 256), 0) == (
        chip * 16 + ((core + (col // 32) % 2) % 2) * 8 + ((col // 8) % 4) * 2 + (col // 64) % 2
    )
    a_cols = dot(a_part, one_hot(pick)).astype(BF16)
    spread = one_hot(chip_of(iota((MR, chips), 0)) == iota((MR, chips), 1))
    rows_a = dot(spread, a_cols)
    for rh in range(2):
        keep = iota((MR, 256), 1) % 8 == rh * 4 + iota((MR, 256), 0) % 4
        m_to[rh] = jnp.where(keep, rows_a, 0.0).astype(BF16)
    row = iota((128, AB), 0)
    pick = base + iota((128, AB), 1) == chip * 16 + ((core + row // 64) % 2) * 8 + (row // 8) % 8
    a_rows = dot(one_hot(pick), a_part, CONTRACT_LAST).astype(BF16)
    spread = one_hot(chip_of(iota((chips, MR), 1)) == iota((chips, MR), 0))
    cols_a = dot(a_rows, spread)
    for rh in range(2):
        keep = iota((128, MR), 0) % 8 == rh * 4 + iota((128, MR), 1) % 4
        m_from[:, rh * MR : (rh + 1) * MR] = jnp.where(keep, cols_a, 0.0).astype(BF16)

    receive(got_b)
    low = low_half((rows_h, 128))
    for i in range(Y):
        v = s_y[i].astype(F32)
        w = swap_halves(v)
        s_all[2 * i * rows_h : (2 * i + 1) * rows_h, :] = jnp.where(low, v, w).astype(BF16)
        s_all[(2 * i + 1) * rows_h : (2 * i + 2) * rows_h, :] = jnp.where(low, w, v).astype(BF16)

    low = low_half((32, 128))
    for cc in range(2):
        t = dot(packed[cc], s_all[...], CONTRACT_FIRST)
        for ah in range(4):
            pair = jnp.where(low, t[ah * 64 : ah * 64 + 32], t[ah * 64 + 32 : ah * 64 + 64])
            for xx in range(4):
                t_out[cc, xx, ah] = pair[xx * 8 : xx * 8 + 8]
    got_t = [
        send(
            t_out.at[(core + dc) % 2, (x + dx) % X],
            t_in.at[dc, dx],
            s_t.at[dc, dx],
            r_t.at[dc, dx],
            at(dx=dx, dc=dc),
        )
        for dc, dx in xc_peers
    ]
    mine = t_out[core, x]
    receive(got_t)
    for dx in range(1, X):
        mine = mine + t_in[0, dx]
    other = t_in[1, 0]
    for dx in range(1, X):
        other = other + t_in[1, dx]
    u = jnp.concatenate([mine.reshape(32, 128), other.reshape(32, 128)], axis=0)
    low = low_half((64, 128))
    v = swap_halves(u)
    u = jnp.concatenate([jnp.where(low, u, v), jnp.where(low, v, u)], axis=0)
    top = u.astype(BF16)
    rest = (u - top.astype(F32)).astype(BF16)
    u = jnp.concatenate([top, rest], axis=0)
    low = low_half((MR, 128))
    part = jnp.where(low, dot(m_to[0], u), dot(m_to[1], u))
    RZ = Y * 4
    for i in range(Z):
        sp_out[i] = part[i * RZ : (i + 1) * RZ].astype(BF16)

    got = [
        send(sp_out.at[(z + dz) % Z], sp_in.at[dz], s_z1.at[dz], r_z1.at[dz], at(dz=dz)) for dz in range(1, Z)
    ]
    total = sp_out[z].astype(F32)
    receive(got)
    for dz in range(1, Z):
        total = total + sp_in[dz].astype(F32)
    z_out[...] = total.astype(BF16)
    got = [send(z_out, z_in.at[dy], s_y1.at[dy], r_y1.at[dy], at(dy=dy)) for dy in range(1, Y)]
    receive(got)
    for dy in range(1, Y):
        total = total + z_in[dy].astype(F32)
    for i in range(Y):
        mz[i] = total[i * 4 : i * 4 + 4]
    s_full[x, z] = total.astype(BF16)
    spot = s_full.at[x, z]
    got = [send(spot, spot, s_z2.at[dz], r_z2.at[dz], at(dz=dz)) for dz in range(1, Z)]
    receive(got)
    spot = s_full.at[x]
    got = [send(spot, spot, s_x1.at[dx], r_x1.at[dx], at(dx=dx)) for dx in range(1, X)]
    receive(got)

    s_x = [s_full[i].reshape(MR, 128) for i in range(X)]
    big = dot(s_x[0], s_x[0], CONTRACT_FIRST)
    for i in range(1, X):
        big = big + dot(s_x[i], s_x[i], CONTRACT_FIRST)
    gram_out[...] = swap_halves(big[0:64]) + big[64:128]
    got_g = send(gram_out, gram_in, s_g, r_g, partner)

    low = low_half((MR, 128))
    rhs = []
    for xp in range(X // 2):
        s0 = s_x[2 * xp].astype(F32)
        s1 = s_x[2 * xp + 1].astype(F32)
        rhs.append(
            jnp.concatenate(
                [jnp.where(low, s0, swap_halves(s1)), jnp.where(low, swap_halves(s0), s1)], axis=0
            ).astype(BF16)
        )
    low = low_half((128, 128))
    for xp in range(X // 2):
        w = dot(m_from[...], rhs[xp])
        v = swap_halves(w)
        even = jnp.where(low, w, v)
        odd = jnp.where(low, v, w)
        for a in range(16):
            w_rows[a, 2 * xp] = even[a * 8 : a * 8 + 8]
            w_rows[a, 2 * xp + 1] = odd[a * 8 : a * 8 + 8]
    receive([got_p])
    w0 = w_rows[0:8].reshape(256, 128).astype(BF16)
    w1 = w_rows[8:16].reshape(256, 128).astype(BF16)
    ylow = dot(packed[core, 0 : FX // 2, :], w0) + dot(packed_in[0 : FX // 2, :], w1)
    yhigh = dot(packed[core, FX // 2 : FX, :], w0) + dot(packed_in[FX // 2 : FX, :], w1)
    ypart = jnp.where(low_half((FX // 2, 128)), ylow, yhigh)
    for i in range(YL):
        for j in range(Z):
            y_out[j, i] = ypart[(i * Z + j) * 8 : (i * Z + j) * 8 + 8]
    got_y = [
        send(y_out.at[(z + dz) % Z], y_in.at[dz], s_yz.at[dz], r_yz.at[dz], at(dz=dz)) for dz in range(1, Z)
    ]

    receive([got_g])
    g = gram_out[...] + gram_in[...]
    low = low_half((64, 128))
    g = jnp.where(low, jnp.where(iota((64, 128), 0) == iota((64, 128), 1), 1.0, 0.0), g)
    tiles = [g[i * 8 : i * 8 + 8] for i in range(8)]
    sub = iota((8, 128), 0)

    def eliminate(tiles, first, last):
        for j in range(first, last):
            pos = j % 8
            line = tiles[j // 8][pos : pos + 1]
            line_scaled = line / line[:, 64 + j : 65 + j]
            for i in range(j // 8, 8):
                c = tiles[i][:, 64 + j : 65 + j]
                if i == j // 8:
                    c = jnp.where(sub[:, 0:1] > pos, c, 0.0)
                tiles[i] = tiles[i] - c * line_scaled
        return tiles

    tiles = eliminate(tiles, 0, 24)

    receive(got_y)
    acc = y_out[z]
    for dz in range(1, Z):
        acc = acc + y_in[dz]
    for i in range(YL):
        for cc in range(2):
            y2_out[i, cc] = acc[i, cc * 4 : cc * 4 + 4]
    got_y = [
        send(
            y2_out.at[((y + dy) % Y) % YL, (core + dc) % 2],
            y2_in.at[dc, dy],
            s_yy.at[dc, dy],
            r_yy.at[dc, dy],
            at(dy=dy, dc=dc),
        )
        for dc, dy in yc_peers
    ]
    tiles = eliminate(tiles, 24, 64)
    x_mat[...] = jnp.concatenate(tiles, axis=0)
    elim = x_mat[...]
    diagonal = jnp.where(iota((64, 128), 1) == iota((64, 128), 0) + 64, elim, 0.0)
    pivots = jnp.sum(diagonal, axis=1, keepdims=True)
    inverse = elim[:, 0:64] * (1.0 / jnp.sqrt(pivots))

    receive(got_y)
    acc = y2_out[y % YL, core]
    for dc, dy in yc_peers:
        acc = acc + y2_in[dc, dy]
    acc = jnp.where(y // YL == 0, acc, swap_halves(acc)) if Y > 1 else acc
    s_mine = mz[y]
    rows = jnp.concatenate([s_mine, swap_halves(s_mine), acc, acc], axis=0)
    out = dot(rows[:, 0:64], inverse, CONTRACT_LAST, lax.Precision.HIGHEST)
    transfer[...] = out[0:8] * float((chips * 64) ** 0.5)
    coefficients[...] = out[8:12]

    for copy in waits:
        copy.wait_send()


def scratch_for(sizes, cb):
    X, Y, Z = sizes
    ZC = Z * 2
    YL = max(Y // 2, 1)
    chips = Y * Z
    FX = chips * 8
    MR = chips * 4
    RZ = Y * 4
    dma = pltpu.SemaphoreType.DMA
    return [
        pltpu.VMEM((8, FX, cb), BF16),
        pltpu.VMEM((FX, 128), F32),
        pltpu.VMEM((2, FX, 256), BF16),
        pltpu.VMEM((FX, 256), BF16),
        pltpu.VMEM((4, 128), F32),
        pltpu.VMEM((ZC, 4, 128), F32),
        pltpu.VMEM((Y, ZC * 2, 128), BF16),
        pltpu.VMEM((FX, 128), BF16),
        pltpu.VMEM((2, 4, 4, 8, 128), F32),
        pltpu.VMEM((2, X, 4, 8, 128), F32),
        pltpu.VMEM((Z, RZ, 128), BF16),
        pltpu.VMEM((Z, RZ, 128), BF16),
        pltpu.VMEM((RZ, 128), BF16),
        pltpu.VMEM((Y, RZ, 128), BF16),
        pltpu.VMEM((Y, 4, 128), F32),
        pltpu.VMEM((X, Z, RZ, 128), BF16),
        pltpu.VMEM((2, MR, 256), BF16),
        pltpu.VMEM((128, 2 * MR), BF16),
        pltpu.VMEM((16, 4, 8, 128), F32),
        pltpu.VMEM((64, 128), F32),
        pltpu.VMEM((64, 128), F32),
        pltpu.VMEM((Z, YL, 8, 128), F32),
        pltpu.VMEM((Z, YL, 8, 128), F32),
        pltpu.VMEM((YL, 2, 4, 128), F32),
        pltpu.VMEM((2, Y, 4, 128), F32),
        pltpu.VMEM((64, 128), F32),
        dma((8,)),
        dma((2, Z)), dma((2, Z)),
        dma((Y,)), dma((Y,)),
        dma, dma,
        dma((2, X)), dma((2, X)),
        dma((Z,)), dma((Z,)),
        dma((Y,)), dma((Y,)),
        dma((Z,)), dma((Z,)),
        dma((X,)), dma((X,)),
        dma, dma,
        dma((Z,)), dma((Z,)),
        dma((2, Y)), dma((2, Y)),
    ]


def per_device(sizes, blocks, basis_a, basis_b, sketch):
    fibres, own_a, cb = blocks.shape
    vmem = pl.BlockSpec(memory_space=pltpu.VMEM)
    return pl.pallas_call(
        functools.partial(kernel, sizes),
        out_shape=(jax.ShapeDtypeStruct((8, 64), F32), jax.ShapeDtypeStruct((4, 64), F32)),
        in_specs=[pl.BlockSpec(memory_space=pl.ANY), vmem, vmem, vmem],
        out_specs=(vmem, vmem),
        scratch_shapes=scratch_for(sizes, cb),
        compiler_params=pltpu.CompilerParams(collective_id=0, has_side_effects=True),
        name="tucker",
    )(blocks.reshape(fibres * own_a, cb), basis_b.T, basis_a.T, sketch)


def solution(mesh):
    chips = mesh.shape["wide"] // 2
    side = int(round(chips ** 0.5))
    sizes = (mesh.shape["pair"], side, chips // side)
    placed = (P("pair", "wide", None), P(), P(), P(("pair", "wide"), None))
    return jax.shard_map(
        functools.partial(per_device, sizes),
        mesh=mesh,
        in_specs=placed,
        out_specs=(P(("wide", "pair"), None), P(("pair", "wide"), None)),
        check_vma=False,
    )
```

```python
import functools

import jax
import jax.numpy as jnp
from jax import lax
from jax.experimental import pallas as pl
from jax.experimental.pallas import tpu as pltpu
from jax.sharding import PartitionSpec as P

MESH = pl.DeviceIdType.MESH
F32 = jnp.float32
BF16 = jnp.bfloat16
CONTRACT_LAST = (((1,), (1,)), ((), ()))
CONTRACT_FIRST = (((0,), (0,)), ((), ()))


def iota(shape, dim):
    return lax.broadcasted_iota(jnp.int32, shape, dim)


def dot(a, b, dims=(((1,), (0,)), ((), ())), precision=None):
    return lax.dot_general(a, b, dims, preferred_element_type=F32, precision=precision)


def low_half(shape):
    return iota(shape, 1) < 64


def swap_halves(v):
    return pltpu.roll(v, 64, 1)


def one_hot(mask):
    return jnp.where(mask, 1.0, 0.0).astype(BF16)


def farthest_first(n):
    return sorted(range(1, n), key=lambda d: -min(d, n - d))


def nearest_first(n):
    return sorted(range(1, n), key=lambda d: min(d, n - d))


def finish(scale, rows, inverse, transfer, coefficients):
    out = dot(rows[:, 0:64], inverse[:, 0:64], CONTRACT_LAST, lax.Precision.HIGHEST)
    transfer[...] = out[0:8] * scale
    coefficients[...] = out[8:12]


def kernel(sizes, blocks, basis_b_in, basis_a_in, sketch_in, rows_out, inverse_out, *scratch):
    X, Y, Z = sizes
    ZC = Z * 2
    YL = max(Y // 2, 1)
    chips = Y * Z
    FX = chips * 8
    FC = FX // 8
    (block_in, wide_n, packed, packed_in, s_own, s_zc, s_y, s_all, t_out, t_in, sp_out, sp_in, z_out, z_in,
     mz, s_full, m_to, m_from, w_rows, gram_out, gram_in, y_out, y_in, y2_out, y2_in, basis_bt, basis_at, sketch,
     in_sem, small_sem, s_a, r_a, s_b, r_b, s_p, r_p, s_t, r_t, s_z1, r_z1, s_y1, r_y1, s_z2, r_z2, s_x1, r_x1,
     s_g, r_g, s_yz, r_yz, s_yy, r_yy) = scratch

    wide = lax.axis_index("wide")
    x = lax.axis_index("pair")
    core = wide % 2
    chip = wide // 2
    z = chip % Z
    y = chip // Z

    def at(dx=0, dy=0, dz=0, dc=0):
        row = ((y + dy) % Y) * Z + (z + dz) % Z
        return (row * 2 + (core + dc) % 2, (x + dx) % X)

    waits = []

    def send(src, dst, ssem, rsem, peer):
        copy = pltpu.make_async_remote_copy(
            src_ref=src, dst_ref=dst, send_sem=ssem, recv_sem=rsem, device_id=peer, device_id_type=MESH
        )
        copy.start()
        waits.append(copy)
        return copy

    def receive(copies):
        for copy in copies:
            copy.wait_recv()

    far_z, far_y, far_x = farthest_first(Z), farthest_first(Y), farthest_first(X)
    zc_peers = [(dc, dz) for dz in far_z + [0] for dc in range(2) if dc or dz]
    yc_peers = [(dc, dy) for dy in far_y + [0] for dc in range(2) if dc or dy]
    xc_peers = [(dc, dx) for dx in far_x + [0] for dc in range(2) if dc or dx]

    barrier = pltpu.get_barrier_semaphore()
    met = 0
    for dc, dz in zc_peers:
        pl.semaphore_signal(barrier, inc=1, device_id=at(dz=dz, dc=dc), device_id_type=MESH)
        met += 1
    for dc, dy in yc_peers:
        if dy:
            pl.semaphore_signal(barrier, inc=1, device_id=at(dy=dy, dc=dc), device_id_type=MESH)
            met += 1
    for dc, dx in xc_peers:
        if dx:
            pl.semaphore_signal(barrier, inc=1, device_id=at(dx=dx, dc=dc), device_id_type=MESH)
            met += 1

    small = [
        pltpu.make_async_copy(src, dst, small_sem.at[i])
        for i, (src, dst) in enumerate(((sketch_in, sketch), (basis_b_in, basis_bt), (basis_a_in, basis_at)))
    ]
    for load in small:
        load.start()
    loads = [
        pltpu.make_async_copy(blocks.at[pl.ds(i * FX, FX)], block_in.at[i], in_sem.at[i]) for i in range(8)
    ]
    for load in loads:
        load.start()

    twice = one_hot(iota((64, 128), 1) % 64 == iota((64, 128), 0))
    small[0].wait()
    s_mine = dot(sketch[...], twice)
    s_own[...] = s_mine
    zc = z * 2 + core
    s_zc[zc] = s_mine
    pl.semaphore_wait(barrier, met)

    got_a = [
        send(s_own, s_zc.at[zc], s_a.at[dc, dz], r_a.at[dc, dz], at(dz=dz, dc=dc)) for dc, dz in zc_peers
    ]

    small[1].wait()
    basis2 = jnp.concatenate([basis_bt[...], basis_bt[...]], axis=0)

    def narrow(i, carry):
        pltpu.make_async_copy(blocks.at[pl.ds(i * FX, FX)], block_in.at[i], in_sem.at[i]).wait()
        wide_n[...] = dot(block_in[i], basis2, CONTRACT_LAST)
        rows = pl.ds(pl.multiple_of(i * FC, FC), FC)
        low = low_half((FC, 128))
        odd = (iota((FC, 128), 1) // 32) % 2 == 1
        for t in range(2):
            part = [wide_n[pl.ds(t * 4 + q, FC, stride=8), :] for q in range(4)]
            first = jnp.where(low, part[0], part[2])
            second = jnp.where(low, part[1], part[3])
            lanes = slice(t * 128, t * 128 + 128)
            packed[0, rows, lanes] = jnp.where(odd, pltpu.roll(second, 32, 1), first).astype(BF16)
            packed[1, rows, lanes] = jnp.where(odd, second, pltpu.roll(first, 96, 1)).astype(BF16)
        return carry

    lax.fori_loop(0, 4, narrow, 0)

    receive(got_a)
    half = ZC // 2
    lo = jnp.concatenate([s_zc[i] for i in range(half)], axis=0)
    hi = jnp.concatenate([s_zc[half + i] for i in range(half)], axis=0)
    rows_h = half * 4
    s_y[y] = jnp.where(low_half((rows_h, 128)), lo, hi).astype(BF16)
    got_b = [send(s_y.at[y], s_y.at[y], s_b.at[dy], r_b.at[dy], at(dy=dy)) for dy in far_y]

    lax.fori_loop(4, 8, narrow, 0)
    partner = at(dc=1)
    got_p = send(packed.at[1 - core], packed_in, s_p, r_p, partner)

    small[2].wait()

    AB = min(chips * 16, 128)
    base = pl.multiple_of((chip * 16 // AB) * AB, AB)
    a_part = basis_at[:, pl.ds(base, AB)]
    MR = chips * 4

    def chip_of(index):
        zy = index // 4
        return (zy % Y) * Z + zy // Y

    col = iota((AB, 256), 1)
    pick = base + iota((AB, 256), 0) == (
        chip * 16 + ((core + (col // 32) % 2) % 2) * 8 + ((col // 8) % 4) * 2 + (col // 64) % 2
    )
    a_cols = dot(a_part, one_hot(pick)).astype(BF16)
    spread = one_hot(chip_of(iota((MR, chips), 0)) == iota((MR, chips), 1))
    rows_a = dot(spread, a_cols)
    for rh in range(2):
        keep = iota((MR, 256), 1) % 8 == rh * 4 + iota((MR, 256), 0) % 4
        m_to[rh] = jnp.where(keep, rows_a, 0.0).astype(BF16)
    row = iota((128, AB), 0)
    pick = base + iota((128, AB), 1) == chip * 16 + ((core + row // 64) % 2) * 8 + (row // 8) % 8
    a_rows = dot(one_hot(pick), a_part, CONTRACT_LAST).astype(BF16)
    spread = one_hot(chip_of(iota((chips, MR), 1)) == iota((chips, MR), 0))
    cols_a = dot(a_rows, spread)
    for rh in range(2):
        keep = iota((128, MR), 0) % 8 == rh * 4 + iota((128, MR), 1) % 4
        m_from[:, rh * MR : (rh + 1) * MR] = jnp.where(keep, cols_a, 0.0).astype(BF16)

    receive(got_b)
    low = low_half((rows_h, 128))
    for i in range(Y):
        v = s_y[i].astype(F32)
        w = swap_halves(v)
        s_all[2 * i * rows_h : (2 * i + 1) * rows_h, :] = jnp.where(low, v, w).astype(BF16)
        s_all[(2 * i + 1) * rows_h : (2 * i + 2) * rows_h, :] = jnp.where(low, w, v).astype(BF16)

    low = low_half((32, 128))
    for cc in range(2):
        t = dot(packed[cc], s_all[...], CONTRACT_FIRST)
        for ah in range(4):
            pair = jnp.where(low, t[ah * 64 : ah * 64 + 32], t[ah * 64 + 32 : ah * 64 + 64])
            for xx in range(4):
                t_out[cc, xx, ah] = pair[xx * 8 : xx * 8 + 8]
    got_t = [
        send(
            t_out.at[(core + dc) % 2, (x + dx) % X],
            t_in.at[dc, dx],
            s_t.at[dc, dx],
            r_t.at[dc, dx],
            at(dx=dx, dc=dc),
        )
        for dc, dx in xc_peers
    ]
    mine = t_out[core, x]
    receive(got_t)
    for dx in range(1, X):
        mine = mine + t_in[0, dx]
    other = t_in[1, 0]
    for dx in range(1, X):
        other = other + t_in[1, dx]
    u = jnp.concatenate([mine.reshape(32, 128), other.reshape(32, 128)], axis=0)
    low = low_half((64, 128))
    v = swap_halves(u)
    u = jnp.concatenate([jnp.where(low, u, v), jnp.where(low, v, u)], axis=0)
    top = u.astype(BF16)
    rest = (u - top.astype(F32)).astype(BF16)
    u = jnp.concatenate([top, rest], axis=0)
    low = low_half((MR, 128))
    part = jnp.where(low, dot(m_to[0], u), dot(m_to[1], u))
    RZ = Y * 4
    for i in range(Z):
        sp_out[i] = part[i * RZ : (i + 1) * RZ].astype(BF16)

    got = [
        send(sp_out.at[(z + dz) % Z], sp_in.at[dz], s_z1.at[dz], r_z1.at[dz], at(dz=dz)) for dz in far_z
    ]
    total = sp_out[z].astype(F32)
    receive(got)
    for dz in range(1, Z):
        total = total + sp_in[dz].astype(F32)
    z_out[...] = total.astype(BF16)
    got = [send(z_out, z_in.at[dy], s_y1.at[dy], r_y1.at[dy], at(dy=dy)) for dy in far_y]
    receive(got)
    for dy in range(1, Y):
        total = total + z_in[dy].astype(F32)
    for i in range(Y):
        mz[i] = total[i * 4 : i * 4 + 4]
    s_full[x, z] = total.astype(BF16)
    spot = s_full.at[x, z]
    got = {dz: send(spot, spot, s_z2.at[dz], r_z2.at[dz], at(dz=dz)) for dz in far_z}
    got_x = []
    for dz in [0] + nearest_first(Z):
        if dz:
            receive([got[dz]])
        spot = s_full.at[x, (z + Z - dz) % Z]
        for dx in far_x:
            got_x.append(send(spot, spot, s_x1.at[dx, dz], r_x1.at[dx, dz], at(dx=dx)))
    receive(got_x)
    s_x = [s_full[i].reshape(MR, 128) for i in range(X)]

    low = low_half((MR, 128))
    rhs = []
    for xp in range(X // 2):
        s0 = s_x[2 * xp].astype(F32)
        s1 = s_x[2 * xp + 1].astype(F32)
        rhs.append(
            jnp.concatenate(
                [jnp.where(low, s0, swap_halves(s1)), jnp.where(low, swap_halves(s0), s1)], axis=0
            ).astype(BF16)
        )
    low = low_half((128, 128))
    for xp in range(X // 2):
        w = dot(m_from[...], rhs[xp])
        v = swap_halves(w)
        even = jnp.where(low, w, v)
        odd = jnp.where(low, v, w)
        for a in range(16):
            w_rows[a, 2 * xp] = even[a * 8 : a * 8 + 8]
            w_rows[a, 2 * xp + 1] = odd[a * 8 : a * 8 + 8]
    receive([got_p])
    w0 = w_rows[0:8].reshape(256, 128).astype(BF16)
    w1 = w_rows[8:16].reshape(256, 128).astype(BF16)
    ylow = dot(packed[core, 0 : FX // 2, :], w0) + dot(packed_in[0 : FX // 2, :], w1)
    yhigh = dot(packed[core, FX // 2 : FX, :], w0) + dot(packed_in[FX // 2 : FX, :], w1)
    ypart = jnp.where(low_half((FX // 2, 128)), ylow, yhigh)
    for j in range(Z):
        block = [ypart[(i * Z + j) * 8 : (i * Z + j) * 8 + 8] for i in range(YL)]
        y_out[j] = jnp.concatenate(block, axis=0).astype(BF16)
    got_y = [send(y_out.at[(z + dz) % Z], y_in.at[dz], s_yz.at[dz], r_yz.at[dz], at(dz=dz)) for dz in far_z]

    big = dot(s_x[0], s_x[0], CONTRACT_FIRST)
    for i in range(1, X):
        big = big + dot(s_x[i], s_x[i], CONTRACT_FIRST)
    gram_out[...] = swap_halves(big[0:64]) + big[64:128]
    got_g = send(gram_out, gram_in, s_g, r_g, partner)

    receive([got_g])
    g = gram_out[...] + gram_in[...]
    low = low_half((64, 128))
    g = jnp.where(low, jnp.where(iota((64, 128), 0) == iota((64, 128), 1), 1.0, 0.0), g)
    tiles = [g[i * 8 : i * 8 + 8] for i in range(8)]
    sub = iota((8, 128), 0)

    def lane(v, j):
        return jnp.broadcast_to(v[:, 64 + j : 65 + j], v.shape)

    def eliminate(tiles, first, last):
        for j in range(first, last, 4):
            home, pos = j // 8, j % 8
            lines = [tiles[home][pos + t : pos + t + 1] for t in range(4)]
            u = [[lane(lines[t], j + v) for v in range(4)] for t in range(4)]
            inv = []
            for t in range(4):
                inv.append(1.0 / u[t][t])
                for v in range(t + 1, 4):
                    ratio = u[t][v] * inv[t]
                    for w in range(v, 4):
                        u[v][w] = u[v][w] - ratio * u[t][w]
                    lines[v] = lines[v] - ratio * lines[t]
            for i in range(home, 8):
                c = [lane(tiles[i], j + v) for v in range(4)]
                new = tiles[i]
                for t in range(4):
                    m = c[t] * inv[t]
                    if i == home:
                        m = jnp.where(sub > pos + t, m, 0.0)
                    for v in range(t + 1, 4):
                        c[v] = c[v] - m * u[t][v]
                    new = new - m * lines[t]
                tiles[i] = new
        return tiles

    tiles = eliminate(tiles, 0, 32)

    receive(got_y)
    acc = y_out[z].astype(F32)
    for dz in range(1, Z):
        acc = acc + y_in[dz].astype(F32)
    for i in range(YL):
        for cc in range(2):
            y2_out[i, cc] = acc[i * 8 + cc * 4 : i * 8 + cc * 4 + 4]
    got_y = [
        send(
            y2_out.at[((y + dy) % Y) % YL, (core + dc) % 2],
            y2_in.at[dc, dy],
            s_yy.at[dc, dy],
            r_yy.at[dc, dy],
            at(dy=dy, dc=dc),
        )
        for dc, dy in yc_peers
    ]
    tiles = eliminate(tiles, 32, 64)
    elim = jnp.concatenate(tiles, axis=0)
    diagonal = jnp.where(iota((64, 128), 1) == iota((64, 128), 0) + 64, elim, 0.0)
    pivots = jnp.sum(diagonal, axis=1, keepdims=True)
    inverse_out[...] = elim * (1.0 / jnp.sqrt(pivots))

    receive(got_y)
    acc = y2_out[y % YL, core]
    for dc, dy in yc_peers:
        acc = acc + y2_in[dc, dy]
    acc = jnp.where(y // YL == 0, acc, swap_halves(acc)) if Y > 1 else acc
    s_mine = mz[y]
    rows_out[...] = jnp.concatenate([s_mine, swap_halves(s_mine), acc, acc], axis=0)

    for copy in waits:
        copy.wait_send()


def scratch_for(sizes, cb):
    X, Y, Z = sizes
    ZC = Z * 2
    YL = max(Y // 2, 1)
    chips = Y * Z
    FX = chips * 8
    MR = chips * 4
    RZ = Y * 4
    dma = pltpu.SemaphoreType.DMA
    return [
        pltpu.VMEM((8, FX, cb), BF16),
        pltpu.VMEM((FX, 128), F32),
        pltpu.VMEM((2, FX, 256), BF16),
        pltpu.VMEM((FX, 256), BF16),
        pltpu.VMEM((4, 128), F32),
        pltpu.VMEM((ZC, 4, 128), F32),
        pltpu.VMEM((Y, ZC * 2, 128), BF16),
        pltpu.VMEM((FX, 128), BF16),
        pltpu.VMEM((2, 4, 4, 8, 128), F32),
        pltpu.VMEM((2, X, 4, 8, 128), F32),
        pltpu.VMEM((Z, RZ, 128), BF16),
        pltpu.VMEM((Z, RZ, 128), BF16),
        pltpu.VMEM((RZ, 128), BF16),
        pltpu.VMEM((Y, RZ, 128), BF16),
        pltpu.VMEM((Y, 4, 128), F32),
        pltpu.VMEM((X, Z, RZ, 128), BF16),
        pltpu.VMEM((2, MR, 256), BF16),
        pltpu.VMEM((128, 2 * MR), BF16),
        pltpu.VMEM((16, 4, 8, 128), F32),
        pltpu.VMEM((64, 128), F32),
        pltpu.VMEM((64, 128), F32),
        pltpu.VMEM((Z, YL * 8, 128), BF16),
        pltpu.VMEM((Z, YL * 8, 128), BF16),
        pltpu.VMEM((YL, 2, 4, 128), F32),
        pltpu.VMEM((2, Y, 4, 128), F32),
        pltpu.VMEM((64, cb), BF16),
        pltpu.VMEM((chips, chips * 16), BF16),
        pltpu.VMEM((4, 64), BF16),
        dma((8,)),
        dma((3,)),
        dma((2, Z)), dma((2, Z)),
        dma((Y,)), dma((Y,)),
        dma, dma,
        dma((2, X)), dma((2, X)),
        dma((Z,)), dma((Z,)),
        dma((Y,)), dma((Y,)),
        dma((Z,)), dma((Z,)),
        dma((X, Z)), dma((X, Z)),
        dma, dma,
        dma((Z,)), dma((Z,)),
        dma((2, Y)), dma((2, Y)),
    ]


def per_device(sizes, blocks, basis_a, basis_b, sketch):
    fibres, own_a, cb = blocks.shape
    vmem = pl.BlockSpec(memory_space=pltpu.VMEM)
    anywhere = pl.BlockSpec(memory_space=pl.ANY)
    rows, inverse = pl.pallas_call(
        functools.partial(kernel, sizes),
        out_shape=(jax.ShapeDtypeStruct((16, 128), F32), jax.ShapeDtypeStruct((64, 128), F32)),
        in_specs=[anywhere] * 4,
        out_specs=(vmem, vmem),
        scratch_shapes=scratch_for(sizes, cb),
        compiler_params=pltpu.CompilerParams(collective_id=0, has_side_effects=True),
        name="tucker",
    )(blocks.reshape(fibres * own_a, cb), basis_b.T, basis_a.T, sketch)
    chips = sizes[1] * sizes[2]
    return pl.pallas_call(
        functools.partial(finish, float((chips * 64) ** 0.5)),
        out_shape=(jax.ShapeDtypeStruct((8, 64), F32), jax.ShapeDtypeStruct((4, 64), F32)),
        in_specs=[vmem, vmem],
        out_specs=(vmem, vmem),
        name="finish",
    )(rows, inverse)


def solution(mesh):
    chips = mesh.shape["wide"] // 2
    side = int(round(chips ** 0.5))
    sizes = (mesh.shape["pair"], side, chips // side)
    placed = (P("pair", "wide", None), P(), P(), P(("pair", "wide"), None))
    return jax.shard_map(
        functools.partial(per_device, sizes),
        mesh=mesh,
        in_specs=placed,
        out_specs=(P(("wide", "pair"), None), P(("pair", "wide"), None)),
        check_vma=False,
    )
```

```python
import functools

import jax
import jax.numpy as jnp
from jax import lax
from jax.experimental import pallas as pl
from jax.experimental.pallas import tpu as pltpu
from jax.sharding import PartitionSpec as P

MESH = pl.DeviceIdType.MESH
F32 = jnp.float32
BF16 = jnp.bfloat16
CONTRACT_LAST = (((1,), (1,)), ((), ()))
CONTRACT_FIRST = (((0,), (0,)), ((), ()))


def iota(shape, dim):
    return lax.broadcasted_iota(jnp.int32, shape, dim)


def dot(a, b, dims=(((1,), (0,)), ((), ())), precision=None):
    return lax.dot_general(a, b, dims, preferred_element_type=F32, precision=precision)


def low_half(shape):
    return iota(shape, 1) < 64


def swap_halves(v):
    return pltpu.roll(v, 64, 1)


def one_hot(mask):
    return jnp.where(mask, 1.0, 0.0).astype(BF16)


def farthest_first(n):
    return sorted(range(1, n), key=lambda d: -min(d, n - d))


def nearest_first(n):
    return sorted(range(1, n), key=lambda d: min(d, n - d))


def finish(scale, rows, inverse, transfer, coefficients):
    out = dot(rows[:, 0:64], inverse[:, 0:64], CONTRACT_LAST, lax.Precision.HIGHEST)
    transfer[...] = out[0:8] * scale
    coefficients[...] = out[8:12]


def kernel(sizes, blocks, basis_b_in, basis_a_in, sketch_in, rows_out, inverse_out, *scratch):
    X, Y, Z = sizes
    ZC = Z * 2
    ZL = Z // 2
    chips = Y * Z
    FX = chips * 8
    FC = FX // Y
    RC = FC * 8
    (block_in, wide_n, packed, n_in, s_own, s_zc, s_y, s_all, t_out, t_in, sp_out, sp_in, z_out, z_in,
     mz, s_full, m_to, m_from, gram_out, gram_in, y_out, y_in, basis_bt, basis_at, sketch,
     in_sem, small_sem, s_a, r_a, s_b, r_b, s_n, r_n, s_t, r_t, s_z1, r_z1, s_y1, r_y1, s_z2, r_z2, s_x1, r_x1,
     s_g, r_g, s_y1z, r_y1z) = scratch

    wide = lax.axis_index("wide")
    x = lax.axis_index("pair")
    core = wide % 2
    chip = wide // 2
    z = chip % Z
    y = chip // Z

    def at(dx=0, dy=0, dz=0, dc=0):
        row = ((y + dy) % Y) * Z + (z + dz) % Z
        return (row * 2 + (core + dc) % 2, (x + dx) % X)

    waits = []
    slow_waits = []

    def send(src, dst, ssem, rsem, peer, slow=False):
        copy = pltpu.make_async_remote_copy(
            src_ref=src, dst_ref=dst, send_sem=ssem, recv_sem=rsem, device_id=peer, device_id_type=MESH
        )
        copy.start()
        (slow_waits if slow else waits).append(copy)
        return copy

    def receive(copies):
        for copy in reversed(copies):
            copy.wait_recv()

    def drain(keep=0):
        done = waits[: len(waits) - keep]
        for copy in done:
            copy.wait_send()
        del waits[: len(done)]

    far_z, far_y, far_x = farthest_first(Z), farthest_first(Y), farthest_first(X)
    zc_peers = [(dc, dz) for dz in far_z + [0] for dc in range(2) if dc or dz]
    yc_peers = [(dc, dy) for dy in far_y + [0] for dc in range(2) if dc or dy]
    xc_peers = [(dc, dx) for dx in far_x + [0] for dc in range(2) if dc or dx]

    barrier = pltpu.get_barrier_semaphore()
    met = 0
    for dc, dz in zc_peers:
        pl.semaphore_signal(barrier, inc=1, device_id=at(dz=dz, dc=dc), device_id_type=MESH)
        met += 1
    for dc, dy in yc_peers:
        if dy:
            pl.semaphore_signal(barrier, inc=1, device_id=at(dy=dy, dc=dc), device_id_type=MESH)
            met += 1
    for dc, dx in xc_peers:
        if dx:
            pl.semaphore_signal(barrier, inc=1, device_id=at(dx=dx, dc=dc), device_id_type=MESH)
            met += 1

    small = [
        pltpu.make_async_copy(src, dst, small_sem.at[i])
        for i, (src, dst) in enumerate(((sketch_in, sketch), (basis_b_in, basis_bt), (basis_a_in, basis_at)))
    ]
    for load in small:
        load.start()
    loads = [
        pltpu.make_async_copy(blocks.at[pl.ds(i * RC, RC)], block_in.at[i], in_sem.at[i]) for i in range(Y)
    ]
    for load in loads:
        load.start()

    twice = one_hot(iota((64, 128), 1) % 64 == iota((64, 128), 0))
    small[0].wait()
    s_mine = dot(sketch[...], twice)
    s_own[...] = s_mine
    zc = z * 2 + core
    s_zc[zc] = s_mine
    small[1].wait()
    basis2 = jnp.concatenate([basis_bt[...], basis_bt[...]], axis=0)

    def narrow(i, carry):
        pltpu.make_async_copy(blocks.at[pl.ds(i * RC, RC)], block_in.at[i], in_sem.at[i]).wait()
        wide_n[...] = dot(block_in[i], basis2, CONTRACT_LAST)
        low = low_half((FC, 128))
        odd = (iota((FC, 128), 1) // 32) % 2 == 1
        for t in range(2):
            part = [wide_n[pl.ds(t * 4 + q, FC, stride=8), :] for q in range(4)]
            first = jnp.where(low, part[0], part[2])
            second = jnp.where(low, part[1], part[3])
            lanes = slice(t * 128, t * 128 + 128)
            packed[0, i, :, lanes] = jnp.where(odd, pltpu.roll(second, 32, 1), first).astype(BF16)
            packed[1, i, :, lanes] = jnp.where(odd, second, pltpu.roll(first, 96, 1)).astype(BF16)
        return carry

    lax.fori_loop(0, Y // 2, narrow, 0)
    pl.semaphore_wait(barrier, met)

    got_a = [
        send(s_own, s_zc.at[zc], s_a.at[dc, dz], r_a.at[dc, dz], at(dz=dz, dc=dc)) for dc, dz in zc_peers
    ]

    lax.fori_loop(Y // 2, Y, narrow, 0)

    receive(got_a)
    half = ZC // 2
    lo = jnp.concatenate([s_zc[i] for i in range(half)], axis=0)
    hi = jnp.concatenate([s_zc[half + i] for i in range(half)], axis=0)
    rows_h = half * 4
    s_y[y] = jnp.where(low_half((rows_h, 128)), lo, hi).astype(BF16)
    got_b = [send(s_y.at[y], s_y.at[y], s_b.at[dy], r_b.at[dy], at(dy=dy)) for dy in far_y]

    partner = at(dc=1)
    small[2].wait()

    ZA = Z * 16
    a_part = basis_at[:, pl.ds(pl.multiple_of(y * ZA, ZA), ZA)]
    MR = chips * 4

    def chip_of(index):
        zy = index // 4
        return (zy % Y) * Z + zy // Y

    col = iota((ZA, 256), 1)
    pick = iota((ZA, 256), 0) == (
        z * 16 + ((core + (col // 32) % 2) % 2) * 8 + ((col // 8) % 4) * 2 + (col // 64) % 2
    )
    a_cols = dot(a_part, one_hot(pick)).astype(BF16)
    spread = one_hot(chip_of(iota((MR, chips), 0)) == iota((MR, chips), 1))
    rows_a = dot(spread, a_cols)
    for rh in range(2):
        keep = iota((MR, 256), 1) % 8 == rh * 4 + iota((MR, 256), 0) % 4
        m_to[rh] = jnp.where(keep, rows_a, 0.0).astype(BF16)

    receive(got_b)
    low = low_half((rows_h, 128))
    for i in range(Y):
        v = s_y[i].astype(F32)
        w = swap_halves(v)
        s_all[2 * i * rows_h : (2 * i + 1) * rows_h, :] = jnp.where(low, v, w).astype(BF16)
        s_all[(2 * i + 1) * rows_h : (2 * i + 2) * rows_h, :] = jnp.where(low, w, v).astype(BF16)

    low = low_half((32, 128))
    for cc in range(2):
        t = dot(packed[cc].reshape(FX, 256), s_all[...], CONTRACT_FIRST)
        for ah in range(4):
            pair = jnp.where(low, t[ah * 64 : ah * 64 + 32], t[ah * 64 + 32 : ah * 64 + 64])
            for xx in range(4):
                t_out[cc, xx, ah] = pair[xx * 8 : xx * 8 + 8]
    got_t = [
        send(
            t_out.at[(core + dc) % 2, (x + dx) % X],
            t_in.at[dc, dx],
            s_t.at[dc, dx],
            r_t.at[dc, dx],
            at(dx=dx, dc=dc),
        )
        for dc, dx in xc_peers
    ]
    def spread_fibres(peers):
        return [
            send(
                packed.at[(core + dc) % 2, (y + dy) % Y],
                n_in.at[dc, dy],
                s_n.at[dc, dy],
                r_n.at[dc, dy],
                at(dy=dy, dc=dc),
                slow=True,
            )
            for dc, dy in peers
        ]

    got_n = spread_fibres([p for p in yc_peers if p[0] == 0])
    mine = t_out[core, x]
    other = None
    drain(len(got_t))
    for (dc, dx), copy in reversed(list(zip(xc_peers, got_t))):
        copy.wait_recv()
        if dc == 0:
            mine = mine + t_in[0, dx]
        else:
            other = t_in[1, dx] if other is None else other + t_in[1, dx]
    u = jnp.concatenate([mine.reshape(32, 128), other.reshape(32, 128)], axis=0)
    low = low_half((64, 128))
    v = swap_halves(u)
    u = jnp.concatenate([jnp.where(low, u, v), jnp.where(low, v, u)], axis=0)
    top = u.astype(BF16)
    rest = (u - top.astype(F32)).astype(BF16)
    u = jnp.concatenate([top, rest], axis=0)
    low = low_half((MR, 128))
    part = jnp.where(low, dot(m_to[0], u), dot(m_to[1], u))
    RZ = Y * 4
    for i in range(Z):
        sp_out[i] = part[i * RZ : (i + 1) * RZ].astype(BF16)

    got = [
        send(sp_out.at[(z + dz) % Z], sp_in.at[dz], s_z1.at[dz], r_z1.at[dz], at(dz=dz)) for dz in far_z
    ]
    total = sp_out[z].astype(F32)
    drain(len(got))

    row = iota((128, ZA), 0)
    pick = one_hot(iota((128, ZA), 1) == z * 16 + ((core + row // 64) % 2) * 8 + (row // 8) % 8)
    spread = one_hot(chip_of(iota((chips, MR), 1)) == iota((chips, MR), 0))
    for dy in range(Y):
        a_part = basis_at[:, pl.ds(pl.multiple_of(((y + Y - dy) % Y) * ZA, ZA), ZA)]
        cols_a = dot(dot(pick, a_part, CONTRACT_LAST).astype(BF16), spread)
        for rh in range(2):
            keep = iota((128, MR), 0) % 8 == rh * 4 + iota((128, MR), 1) % 4
            m_from[dy * 128 : dy * 128 + 128, rh * MR : (rh + 1) * MR] = jnp.where(keep, cols_a, 0.0).astype(BF16)

    for dz, copy in reversed(list(zip(far_z, got))):
        copy.wait_recv()
        total = total + sp_in[dz].astype(F32)
    z_out[...] = total.astype(BF16)
    got = [send(z_out, z_in.at[dy], s_y1.at[dy], r_y1.at[dy], at(dy=dy)) for dy in far_y]
    drain(len(got))
    for dy, copy in reversed(list(zip(far_y, got))):
        copy.wait_recv()
        total = total + z_in[dy].astype(F32)
    for i in range(Y):
        mz[i] = total[i * 4 : i * 4 + 4]
    s_full[x, z] = total.astype(BF16)
    spot = s_full.at[x, z]
    got = {dz: send(spot, spot, s_z2.at[dz], r_z2.at[dz], at(dz=dz)) for dz in far_z}
    got_n += spread_fibres([p for p in yc_peers if p[0] == 1])
    got_x = []
    drain(len(got))
    for dz in [0] + nearest_first(Z):
        if dz:
            receive([got[dz]])
        spot = s_full.at[x, (z + Z - dz) % Z]
        for dx in far_x:
            got_x.append(send(spot, spot, s_x1.at[dx, dz], r_x1.at[dx, dz], at(dx=dx)))
    drain(len(got_x))
    receive(got_n)
    for i in range(0, len(got_x), len(far_x)):
        receive(got_x[i : i + len(far_x)])
    s_x = [s_full[i].reshape(MR, 128) for i in range(X)]

    big = dot(s_x[0], s_x[0], CONTRACT_FIRST)
    for i in range(1, X):
        big = big + dot(s_x[i], s_x[i], CONTRACT_FIRST)
    gram_out[...] = swap_halves(big[0:64]) + big[64:128]
    got_g = send(gram_out, gram_in, s_g, r_g, partner)

    low = low_half((MR, 128))
    rhs = []
    for xp in range(X // 2):
        s0 = s_x[2 * xp].astype(F32)
        s1 = s_x[2 * xp + 1].astype(F32)
        rhs.append(
            jnp.concatenate(
                [jnp.where(low, s0, swap_halves(s1)), jnp.where(low, swap_halves(s0), s1)], axis=0
            ).astype(BF16)
        )
    w = dot(m_from[...], jnp.concatenate(rhs, axis=1))
    low = low_half((128, 128))
    ypart = None
    for dy in range(Y):
        by_x = []
        for xp in range(X // 2):
            v = w[dy * 128 : dy * 128 + 128, xp * 128 : xp * 128 + 128]
            t = swap_halves(v)
            by_x += [jnp.where(low, v, t), jnp.where(low, t, v)]
        for dc in range(2):
            tiles = [by_x[xx][a * 8 : a * 8 + 8] for a in range(dc * 8, dc * 8 + 8) for xx in range(X)]
            w_rows = jnp.concatenate(tiles, axis=0).astype(BF16)
            fibres = n_in[dc, dy] if dc or dy else packed[core, y]
            term = dot(fibres, w_rows)
            ypart = term if ypart is None else ypart + term
    ypart = jnp.where(low_half((FC // 2, 128)), ypart[0 : FC // 2], ypart[FC // 2 : FC])
    for i in range(ZL):
        for cc in range(2):
            y_out[i, cc] = ypart[i * 8 + cc * 4 : i * 8 + cc * 4 + 4]
    got_y = [
        send(
            y_out.at[((z + dz) % Z) % ZL, (core + dc) % 2],
            y_in.at[dc, dz],
            s_y1z.at[dc, dz],
            r_y1z.at[dc, dz],
            at(dz=dz, dc=dc),
        )
        for dc, dz in zc_peers
    ]

    receive([got_g])
    g = gram_out[...] + gram_in[...]
    low = low_half((64, 128))
    g = jnp.where(low, jnp.where(iota((64, 128), 0) == iota((64, 128), 1), 1.0, 0.0), g)
    tiles = [g[i * 8 : i * 8 + 8] for i in range(8)]
    sub = iota((8, 128), 0)

    def lane(v, j):
        return jnp.broadcast_to(v[:, 64 + j : 65 + j], v.shape)

    def eliminate(tiles, first, last):
        for j in range(first, last, 4):
            home, pos = j // 8, j % 8
            lines = [tiles[home][pos + t : pos + t + 1] for t in range(4)]
            u = [[lane(lines[t], j + v) for v in range(4)] for t in range(4)]
            inv = []
            for t in range(4):
                inv.append(1.0 / u[t][t])
                for v in range(t + 1, 4):
                    ratio = u[t][v] * inv[t]
                    for w in range(v, 4):
                        u[v][w] = u[v][w] - ratio * u[t][w]
                    lines[v] = lines[v] - ratio * lines[t]
            for i in range(home, 8):
                c = [lane(tiles[i], j + v) for v in range(4)]
                new = tiles[i]
                for t in range(4):
                    m = c[t] * inv[t]
                    if i == home:
                        m = jnp.where(sub > pos + t, m, 0.0)
                    for v in range(t + 1, 4):
                        c[v] = c[v] - m * u[t][v]
                    new = new - m * lines[t]
                tiles[i] = new
        return tiles

    tiles = eliminate(tiles, 0, 64)
    elim = jnp.concatenate(tiles, axis=0)
    diagonal = jnp.where(iota((64, 128), 1) == iota((64, 128), 0) + 64, elim, 0.0)
    pivots = jnp.sum(diagonal, axis=1, keepdims=True)
    inverse_out[...] = elim * (1.0 / jnp.sqrt(pivots))

    drain()
    for copy in slow_waits:
        copy.wait_send()
    acc = y_out[z % ZL, core]
    for (dc, dz), copy in reversed(list(zip(zc_peers, got_y))):
        copy.wait_recv()
        acc = acc + y_in[dc, dz]
    acc = jnp.where(z // ZL == 0, acc, swap_halves(acc))
    s_mine = mz[y]
    rows_out[...] = jnp.concatenate([s_mine, swap_halves(s_mine), acc, acc], axis=0)


def scratch_for(sizes, cb):
    X, Y, Z = sizes
    ZC = Z * 2
    ZL = Z // 2
    chips = Y * Z
    FX = chips * 8
    FC = FX // Y
    MR = chips * 4
    RZ = Y * 4
    dma = pltpu.SemaphoreType.DMA
    return [
        pltpu.VMEM((Y, FC * 8, cb), BF16),
        pltpu.VMEM((FC * 8, 128), F32),
        pltpu.VMEM((2, Y, FC, 256), BF16),
        pltpu.VMEM((2, Y, FC, 256), BF16),
        pltpu.VMEM((4, 128), F32),
        pltpu.VMEM((ZC, 4, 128), F32),
        pltpu.VMEM((Y, ZC * 2, 128), BF16),
        pltpu.VMEM((FX, 128), BF16),
        pltpu.VMEM((2, 4, 4, 8, 128), F32),
        pltpu.VMEM((2, X, 4, 8, 128), F32),
        pltpu.VMEM((Z, RZ, 128), BF16),
        pltpu.VMEM((Z, RZ, 128), BF16),
        pltpu.VMEM((RZ, 128), BF16),
        pltpu.VMEM((Y, RZ, 128), BF16),
        pltpu.VMEM((Y, 4, 128), F32),
        pltpu.VMEM((X, Z, RZ, 128), BF16),
        pltpu.VMEM((2, MR, 256), BF16),
        pltpu.VMEM((Y * 128, 2 * MR), BF16),
        pltpu.VMEM((64, 128), F32),
        pltpu.VMEM((64, 128), F32),
        pltpu.VMEM((ZL, 2, 4, 128), F32),
        pltpu.VMEM((2, Z, 4, 128), F32),
        pltpu.VMEM((64, cb), BF16),
        pltpu.VMEM((chips, chips * 16), BF16),
        pltpu.VMEM((4, 64), BF16),
        dma((Y,)),
        dma((3,)),
        dma((2, Z)), dma((2, Z)),
        dma((Y,)), dma((Y,)),
        dma((2, Y)), dma((2, Y)),
        dma((2, X)), dma((2, X)),
        dma((Z,)), dma((Z,)),
        dma((Y,)), dma((Y,)),
        dma((Z,)), dma((Z,)),
        dma((X, Z)), dma((X, Z)),
        dma, dma,
        dma((2, Z)), dma((2, Z)),
    ]


def per_device(sizes, blocks, basis_a, basis_b, sketch):
    fibres, own_a, cb = blocks.shape
    vmem = pl.BlockSpec(memory_space=pltpu.VMEM)
    anywhere = pl.BlockSpec(memory_space=pl.ANY)
    rows, inverse = pl.pallas_call(
        functools.partial(kernel, sizes),
        out_shape=(jax.ShapeDtypeStruct((16, 128), F32), jax.ShapeDtypeStruct((64, 128), F32)),
        in_specs=[anywhere] * 4,
        out_specs=(vmem, vmem),
        scratch_shapes=scratch_for(sizes, cb),
        compiler_params=pltpu.CompilerParams(collective_id=0, has_side_effects=True),
        name="tucker",
    )(blocks.reshape(fibres * own_a, cb), basis_b.T, basis_a.T, sketch)
    chips = sizes[1] * sizes[2]
    return pl.pallas_call(
        functools.partial(finish, float((chips * 64) ** 0.5)),
        out_shape=(jax.ShapeDtypeStruct((8, 64), F32), jax.ShapeDtypeStruct((4, 64), F32)),
        in_specs=[vmem, vmem],
        out_specs=(vmem, vmem),
        name="finish",
    )(rows, inverse)


def solution(mesh):
    chips = mesh.shape["wide"] // 2
    side = int(round(chips ** 0.5))
    sizes = (mesh.shape["pair"], side, chips // side)
    placed = (P("pair", "wide", None), P(), P(), P(("pair", "wide"), None))
    return jax.shard_map(
        functools.partial(per_device, sizes),
        mesh=mesh,
        in_specs=placed,
        out_specs=(P(("wide", "pair"), None), P(("pair", "wide"), None)),
        check_vma=False,
    )
```

```python
import functools

import jax
import jax.numpy as jnp
from jax import lax
from jax.experimental import pallas as pl
from jax.experimental.pallas import tpu as pltpu
from jax.sharding import PartitionSpec as P

MESH = pl.DeviceIdType.MESH
F32 = jnp.float32
BF16 = jnp.bfloat16
CONTRACT_LAST = (((1,), (1,)), ((), ()))
CONTRACT_FIRST = (((0,), (0,)), ((), ()))


def iota(shape, dim):
    return lax.broadcasted_iota(jnp.int32, shape, dim)


def dot(a, b, dims=(((1,), (0,)), ((), ())), precision=None):
    return lax.dot_general(a, b, dims, preferred_element_type=F32, precision=precision)


def low_half(shape):
    return iota(shape, 1) < 64


def swap_halves(v):
    return pltpu.roll(v, 64, 1)


def one_hot(mask):
    return jnp.where(mask, 1.0, 0.0).astype(BF16)


def farthest_first(n):
    return sorted(range(1, n), key=lambda d: -min(d, n - d))


def nearest_first(n):
    return sorted(range(1, n), key=lambda d: min(d, n - d))


def finish(scale, rows, inverse, transfer, coefficients):
    out = dot(rows[:, 0:64], inverse[:, 0:64], CONTRACT_LAST, lax.Precision.HIGHEST)
    transfer[...] = out[0:8] * scale
    coefficients[...] = out[8:12]


def kernel(sizes, blocks, basis_b_in, basis_a_in, sketch_in, rows_out, inverse_out, *scratch):
    X, Y, Z = sizes
    ZC = Z * 2
    ZL = Z // 2
    chips = Y * Z
    FX = chips * 8
    FC = FX // Y
    RC = FC * 8
    (block_in, wide_n, by_a, packed, n_in, n_x, s_own, s_zc, s_y, s_all, t_out, t_in, sp_out, sp_in, z_out, z_in,
     mz, s_full, m_to, m_from, gram_out, gram_in, y_out, y_in, basis_bt, basis_at, sketch,
     in_sem, small_sem, s_a, r_a, s_b, r_b, s_n, r_n, s_t, r_t, s_z1, r_z1, s_y1, r_y1, s_z2, r_z2, s_x1, r_x1,
     s_g, r_g, s_y1z, r_y1z) = scratch

    wide = lax.axis_index("wide")
    x = lax.axis_index("pair")
    core = wide % 2
    chip = wide // 2
    z = chip % Z
    y = chip // Z

    def at(dx=0, dy=0, dz=0, dc=0):
        row = ((y + dy) % Y) * Z + (z + dz) % Z
        return (row * 2 + (core + dc) % 2, (x + dx) % X)

    waits = []
    slow_waits = []

    def send(src, dst, ssem, rsem, peer, slow=False):
        copy = pltpu.make_async_remote_copy(
            src_ref=src, dst_ref=dst, send_sem=ssem, recv_sem=rsem, device_id=peer, device_id_type=MESH
        )
        copy.start()
        (slow_waits if slow else waits).append(copy)
        return copy

    def receive(copies):
        for copy in reversed(copies):
            copy.wait_recv()

    def drain(keep=0):
        done = waits[: len(waits) - keep]
        for copy in done:
            copy.wait_send()
        del waits[: len(done)]

    far_z, far_y, far_x = farthest_first(Z), farthest_first(Y), farthest_first(X)
    zc_peers = [(dc, dz) for dz in far_z + [0] for dc in range(2) if dc or dz]
    yc_peers = [(dc, dy) for dy in far_y + [0] for dc in range(2) if dc or dy]
    xc_peers = [(dc, dx) for dx in far_x + [0] for dc in range(2) if dc or dx]

    small = [
        pltpu.make_async_copy(src, dst, small_sem.at[i])
        for i, (src, dst) in enumerate(((sketch_in, sketch), (basis_b_in, basis_bt), (basis_a_in, basis_at)))
    ]
    small[0].start()
    barrier = pltpu.get_barrier_semaphore()
    met = 0
    for dc, dz in zc_peers:
        pl.semaphore_signal(barrier, inc=1, device_id=at(dz=dz, dc=dc), device_id_type=MESH)
        met += 1
    for dc, dy in yc_peers:
        if dy:
            pl.semaphore_signal(barrier, inc=1, device_id=at(dy=dy, dc=dc), device_id_type=MESH)
            met += 1
    for dc, dx in xc_peers:
        if dx:
            pl.semaphore_signal(barrier, inc=1, device_id=at(dx=dx, dc=dc), device_id_type=MESH)
            met += 1

    for load in small[1:]:
        load.start()
    loads = [
        pltpu.make_async_copy(blocks.at[pl.ds(i * RC, RC)], block_in.at[i], in_sem.at[i]) for i in range(Y)
    ]
    for load in loads:
        load.start()

    twice = one_hot(iota((64, 128), 1) % 64 == iota((64, 128), 0))
    small[0].wait()
    s_mine = dot(sketch[...], twice)
    s_own[...] = s_mine
    zc = z * 2 + core
    s_zc[zc] = s_mine
    small[1].wait()
    basis2 = jnp.concatenate([basis_bt[...], basis_bt[...]], axis=0)

    def narrow(i, carry):
        pltpu.make_async_copy(blocks.at[pl.ds(i * RC, RC)], block_in.at[i], in_sem.at[i]).wait()
        wide_n[...] = dot(block_in[i], basis2, CONTRACT_LAST)
        low = low_half((FC, 128))
        odd = (iota((FC, 128), 1) // 32) % 2 == 1
        for t in range(2):
            part = [wide_n[pl.ds(t * 4 + q, FC, stride=8), :] for q in range(4)]
            first = jnp.where(low, part[0], part[2])
            second = jnp.where(low, part[1], part[3])
            lanes = slice(t * 128, t * 128 + 128)
            by_a[0, i, :, lanes] = jnp.where(odd, pltpu.roll(second, 32, 1), first).astype(BF16)
            by_a[1, i, :, lanes] = jnp.where(odd, second, pltpu.roll(first, 96, 1)).astype(BF16)
        return carry

    pl.semaphore_wait(barrier, met)

    got_a = [
        send(s_own, s_zc.at[zc], s_a.at[dc, dz], r_a.at[dc, dz], at(dz=dz, dc=dc)) for dc, dz in zc_peers
    ]

    lax.fori_loop(0, Y, narrow, 0)

    receive(got_a)
    half = ZC // 2
    lo = jnp.concatenate([s_zc[i] for i in range(half)], axis=0)
    hi = jnp.concatenate([s_zc[half + i] for i in range(half)], axis=0)
    rows_h = half * 4
    s_y[y] = jnp.where(low_half((rows_h, 128)), lo, hi).astype(BF16)
    got_b = [send(s_y.at[y], s_y.at[y], s_b.at[dy], r_b.at[dy], at(dy=dy)) for dy in far_y]

    partner = at(dc=1)
    small[2].wait()

    lane_in = iota((256, 256), 0)
    move = one_hot(iota((256, 256), 1) == (lane_in // 8 % 4) * 64 + lane_in // 32 * 8 + lane_in % 8)
    for cc in range(2):
        packed[cc] = dot(by_a[cc].reshape(FX, 256), move).astype(BF16).reshape(Y, FC, 256)

    ZA = Z * 16
    a_part = basis_at[:, pl.ds(pl.multiple_of(y * ZA, ZA), ZA)]
    MR = chips * 4

    def chip_of(index):
        zy = index // 4
        return (zy % Y) * Z + zy // Y

    col = iota((ZA, 256), 1)
    pick = iota((ZA, 256), 0) == (
        z * 16 + ((core + (col // 32) % 2) % 2) * 8 + ((col // 8) % 4) * 2 + (col // 64) % 2
    )
    a_cols = dot(a_part, one_hot(pick)).astype(BF16)
    spread = one_hot(chip_of(iota((MR, chips), 0)) == iota((MR, chips), 1))
    rows_a = dot(spread, a_cols)
    for rh in range(2):
        keep = iota((MR, 256), 1) % 8 == rh * 4 + iota((MR, 256), 0) % 4
        m_to[rh] = jnp.where(keep, rows_a, 0.0).astype(BF16)

    receive(got_b)
    low = low_half((rows_h, 128))
    for i in range(Y):
        v = s_y[i].astype(F32)
        w = swap_halves(v)
        s_all[2 * i * rows_h : (2 * i + 1) * rows_h, :] = jnp.where(low, v, w).astype(BF16)
        s_all[(2 * i + 1) * rows_h : (2 * i + 2) * rows_h, :] = jnp.where(low, w, v).astype(BF16)

    low = low_half((8, 128))
    for cc in range(2):
        t = dot(packed[cc].reshape(FX, 256), s_all[...], CONTRACT_FIRST)
        for xx in range(4):
            for ah in range(4):
                at_a = xx * 64 + ah * 16
                t_out[cc, xx, ah] = jnp.where(low, t[at_a : at_a + 8], t[at_a + 8 : at_a + 16])
    got_t = [
        send(
            t_out.at[(core + dc) % 2, (x + dx) % X],
            t_in.at[dc, dx],
            s_t.at[dc, dx],
            r_t.at[dc, dx],
            at(dx=dx, dc=dc),
        )
        for dc, dx in xc_peers
    ]
    def spread_fibres(peers):
        return [
            send(
                packed.at[(core + dc) % 2, (y + dy) % Y],
                n_in.at[dc, dy],
                s_n.at[dc, dy],
                r_n.at[dc, dy],
                at(dy=dy, dc=dc),
                slow=True,
            )
            for dc, dy in peers
        ]

    got_n = spread_fibres([p for p in yc_peers if p[0] == 0])
    mine = t_out[core, x]
    other = None
    drain(len(got_t))
    for (dc, dx), copy in reversed(list(zip(xc_peers, got_t))):
        copy.wait_recv()
        if dc == 0:
            mine = mine + t_in[0, dx]
        else:
            other = t_in[1, dx] if other is None else other + t_in[1, dx]
    u = jnp.concatenate([mine.reshape(32, 128), other.reshape(32, 128)], axis=0)
    low = low_half((64, 128))
    v = swap_halves(u)
    u = jnp.concatenate([jnp.where(low, u, v), jnp.where(low, v, u)], axis=0)
    top = u.astype(BF16)
    rest = (u - top.astype(F32)).astype(BF16)
    u = jnp.concatenate([top, rest], axis=0)
    low = low_half((MR, 128))
    part = jnp.where(low, dot(m_to[0], u), dot(m_to[1], u))
    RZ = Y * 4
    for i in range(Z):
        sp_out[i] = part[i * RZ : (i + 1) * RZ].astype(BF16)

    got = [
        send(sp_out.at[(z + dz) % Z], sp_in.at[dz], s_z1.at[dz], r_z1.at[dz], at(dz=dz)) for dz in far_z
    ]
    total = sp_out[z].astype(F32)
    drain(len(got))

    row = iota((128, ZA), 0)
    pick = one_hot(iota((128, ZA), 1) == z * 16 + ((core + row // 64) % 2) * 8 + (row // 8) % 8)
    spread = one_hot(chip_of(iota((chips, MR), 1)) == iota((chips, MR), 0))
    for dy in range(Y):
        a_part = basis_at[:, pl.ds(pl.multiple_of(((y + Y - dy) % Y) * ZA, ZA), ZA)]
        cols_a = dot(dot(pick, a_part, CONTRACT_LAST).astype(BF16), spread)
        for rh in range(2):
            keep = iota((128, MR), 0) % 8 == rh * 4 + iota((128, MR), 1) % 4
            m_from[dy * 128 : dy * 128 + 128, rh * MR : (rh + 1) * MR] = jnp.where(keep, cols_a, 0.0).astype(BF16)

    for dz, copy in reversed(list(zip(far_z, got))):
        copy.wait_recv()
        total = total + sp_in[dz].astype(F32)
    z_out[...] = total.astype(BF16)
    got = [send(z_out, z_in.at[dy], s_y1.at[dy], r_y1.at[dy], at(dy=dy)) for dy in far_y]
    drain(len(got))
    for dy, copy in reversed(list(zip(far_y, got))):
        copy.wait_recv()
        total = total + z_in[dy].astype(F32)
    for i in range(Y):
        mz[i] = total[i * 4 : i * 4 + 4]
    s_full[x, z] = total.astype(BF16)
    spot = s_full.at[x, z]
    got = {dz: send(spot, spot, s_z2.at[dz], r_z2.at[dz], at(dz=dz)) for dz in far_z}
    got_n += spread_fibres([p for p in yc_peers if p[0] == 1])
    got_x = []
    drain(len(got))
    for dz in [0] + nearest_first(Z):
        if dz:
            receive([got[dz]])
        spot = s_full.at[x, (z + Z - dz) % Z]
        for dx in far_x:
            got_x.append(send(spot, spot, s_x1.at[dx, dz], r_x1.at[dx, dz], at(dx=dx)))
    drain(len(got_x))

    def block_of(xx):
        rows = s_full[xx].reshape(MR, 128)
        return rows, dot(rows, rows, CONTRACT_FIRST)

    low = low_half((MR, 128))

    def back(rows):
        wide_s = rows.astype(F32)
        turned = swap_halves(wide_s)
        both = jnp.concatenate([jnp.where(low, wide_s, turned), jnp.where(low, turned, wide_s)], axis=0)
        return dot(m_from[...], both.astype(BF16)).astype(BF16)

    rows, big = block_of(x)
    w_rows = back(rows)

    receive(got_n)
    half = low_half((FC, 128))
    for dy in range(Y):
        own = (n_in[0, dy] if dy else packed[core, y]).astype(F32)
        other = n_in[1, dy].astype(F32)
        spot = slice(dy * 128, dy * 128 + 128)
        for xp in range(X // 2):
            a_side = own[:, xp * 128 : xp * 128 + 128]
            b_side = other[:, xp * 128 : xp * 128 + 128]
            n_x[2 * xp, :, spot] = jnp.where(half, a_side, swap_halves(b_side)).astype(BF16)
            n_x[2 * xp + 1, :, spot] = jnp.where(half, swap_halves(a_side), b_side).astype(BF16)
    ypart = dot(n_x[x], w_rows)
    near_x = nearest_first(X)
    for dx in near_x:
        receive(got_x[far_x.index(dx) :: len(far_x)])
        xx = (x + X - dx) % X
        rows, more = block_of(xx)
        big = big + more
        if dx == near_x[-1]:
            gram_out[...] = swap_halves(big[0:64]) + big[64:128]
            got_g = send(gram_out, gram_in, s_g, r_g, partner)
        ypart = ypart + dot(n_x[xx], back(rows))
    ypart = jnp.where(low_half((FC // 2, 128)), ypart[0 : FC // 2], ypart[FC // 2 : FC])
    for i in range(ZL):
        for cc in range(2):
            y_out[i, cc] = ypart[i * 8 + cc * 4 : i * 8 + cc * 4 + 4]
    got_y = [
        send(
            y_out.at[((z + dz) % Z) % ZL, (core + dc) % 2],
            y_in.at[dc, dz],
            s_y1z.at[dc, dz],
            r_y1z.at[dc, dz],
            at(dz=dz, dc=dc),
        )
        for dc, dz in zc_peers
    ]

    receive([got_g])
    g = gram_out[...] + gram_in[...]
    low = low_half((64, 128))
    g = jnp.where(low, jnp.where(iota((64, 128), 0) == iota((64, 128), 1), 1.0, 0.0), g)
    tiles = [g[i * 8 : i * 8 + 8] for i in range(8)]
    sub = iota((8, 128), 0)

    def lane(v, j):
        return jnp.broadcast_to(v[:, 64 + j : 65 + j], v.shape)

    def eliminate(tiles, first, last):
        for j in range(first, last, 4):
            home, pos = j // 8, j % 8
            lines = [tiles[home][pos + t : pos + t + 1] for t in range(4)]
            u = [[lane(lines[t], j + v) for v in range(4)] for t in range(4)]
            inv = []
            for t in range(4):
                inv.append(1.0 / u[t][t])
                for v in range(t + 1, 4):
                    ratio = u[t][v] * inv[t]
                    for w in range(v, 4):
                        u[v][w] = u[v][w] - ratio * u[t][w]
                    lines[v] = lines[v] - ratio * lines[t]
            for i in range(home, 8):
                c = [lane(tiles[i], j + v) for v in range(4)]
                new = tiles[i]
                for t in range(4):
                    m = c[t] * inv[t]
                    if i == home:
                        m = jnp.where(sub > pos + t, m, 0.0)
                    for v in range(t + 1, 4):
                        c[v] = c[v] - m * u[t][v]
                    new = new - m * lines[t]
                tiles[i] = new
        return tiles

    tiles = eliminate(tiles, 0, 64)
    elim = jnp.concatenate(tiles, axis=0)
    diagonal = jnp.where(iota((64, 128), 1) == iota((64, 128), 0) + 64, elim, 0.0)
    pivots = jnp.sum(diagonal, axis=1, keepdims=True)
    inverse_out[...] = elim * (1.0 / jnp.sqrt(pivots))

    drain()
    for copy in slow_waits:
        copy.wait_send()
    acc = y_out[z % ZL, core]
    for (dc, dz), copy in reversed(list(zip(zc_peers, got_y))):
        copy.wait_recv()
        acc = acc + y_in[dc, dz]
    acc = jnp.where(z // ZL == 0, acc, swap_halves(acc))
    s_mine = mz[y]
    rows_out[...] = jnp.concatenate([s_mine, swap_halves(s_mine), acc, acc], axis=0)


def scratch_for(sizes, cb):
    X, Y, Z = sizes
    ZC = Z * 2
    ZL = Z // 2
    chips = Y * Z
    FX = chips * 8
    FC = FX // Y
    MR = chips * 4
    RZ = Y * 4
    dma = pltpu.SemaphoreType.DMA
    return [
        pltpu.VMEM((Y, FC * 8, cb), BF16),
        pltpu.VMEM((FC * 8, 128), F32),
        pltpu.VMEM((2, Y, FC, 256), BF16),
        pltpu.VMEM((2, Y, FC, 256), BF16),
        pltpu.VMEM((2, Y, FC, 256), BF16),
        pltpu.VMEM((X, FC, Y * 128), BF16),
        pltpu.VMEM((4, 128), F32),
        pltpu.VMEM((ZC, 4, 128), F32),
        pltpu.VMEM((Y, ZC * 2, 128), BF16),
        pltpu.VMEM((FX, 128), BF16),
        pltpu.VMEM((2, 4, 4, 8, 128), F32),
        pltpu.VMEM((2, X, 4, 8, 128), F32),
        pltpu.VMEM((Z, RZ, 128), BF16),
        pltpu.VMEM((Z, RZ, 128), BF16),
        pltpu.VMEM((RZ, 128), BF16),
        pltpu.VMEM((Y, RZ, 128), BF16),
        pltpu.VMEM((Y, 4, 128), F32),
        pltpu.VMEM((X, Z, RZ, 128), BF16),
        pltpu.VMEM((2, MR, 256), BF16),
        pltpu.VMEM((Y * 128, 2 * MR), BF16),
        pltpu.VMEM((64, 128), F32),
        pltpu.VMEM((64, 128), F32),
        pltpu.VMEM((ZL, 2, 4, 128), F32),
        pltpu.VMEM((2, Z, 4, 128), F32),
        pltpu.VMEM((64, cb), BF16),
        pltpu.VMEM((chips, chips * 16), BF16),
        pltpu.VMEM((4, 64), BF16),
        dma((Y,)),
        dma((3,)),
        dma((2, Z)), dma((2, Z)),
        dma((Y,)), dma((Y,)),
        dma((2, Y)), dma((2, Y)),
        dma((2, X)), dma((2, X)),
        dma((Z,)), dma((Z,)),
        dma((Y,)), dma((Y,)),
        dma((Z,)), dma((Z,)),
        dma((X, Z)), dma((X, Z)),
        dma, dma,
        dma((2, Z)), dma((2, Z)),
    ]


def per_device(sizes, blocks, basis_a, basis_b, sketch):
    fibres, own_a, cb = blocks.shape
    vmem = pl.BlockSpec(memory_space=pltpu.VMEM)
    anywhere = pl.BlockSpec(memory_space=pl.ANY)
    rows, inverse = pl.pallas_call(
        functools.partial(kernel, sizes),
        out_shape=(jax.ShapeDtypeStruct((16, 128), F32), jax.ShapeDtypeStruct((64, 128), F32)),
        in_specs=[anywhere] * 4,
        out_specs=(vmem, vmem),
        scratch_shapes=scratch_for(sizes, cb),
        compiler_params=pltpu.CompilerParams(collective_id=0, has_side_effects=True),
        name="tucker",
    )(blocks.reshape(fibres * own_a, cb), basis_b.T, basis_a.T, sketch)
    chips = sizes[1] * sizes[2]
    return pl.pallas_call(
        functools.partial(finish, float((chips * 64) ** 0.5)),
        out_shape=(jax.ShapeDtypeStruct((8, 64), F32), jax.ShapeDtypeStruct((4, 64), F32)),
        in_specs=[vmem, vmem],
        out_specs=(vmem, vmem),
        name="finish",
    )(rows, inverse)


def solution(mesh):
    chips = mesh.shape["wide"] // 2
    side = int(round(chips ** 0.5))
    sizes = (mesh.shape["pair"], side, chips // side)
    placed = (P("pair", "wide", None), P(), P(), P(("pair", "wide"), None))
    return jax.shard_map(
        functools.partial(per_device, sizes),
        mesh=mesh,
        in_specs=placed,
        out_specs=(P(("wide", "pair"), None), P(("pair", "wide"), None)),
        check_vma=False,
    )
```

```python
import functools

import jax
import jax.numpy as jnp
from jax import lax
from jax.experimental import pallas as pl
from jax.experimental.pallas import tpu as pltpu
from jax.sharding import PartitionSpec as P

MESH = pl.DeviceIdType.MESH
F32 = jnp.float32
BF16 = jnp.bfloat16
CONTRACT_LAST = (((1,), (1,)), ((), ()))
CONTRACT_FIRST = (((0,), (0,)), ((), ()))


def iota(shape, dim):
    return lax.broadcasted_iota(jnp.int32, shape, dim)


def dot(a, b, dims=(((1,), (0,)), ((), ())), precision=None):
    return lax.dot_general(a, b, dims, preferred_element_type=F32, precision=precision)


def low_half(shape):
    return iota(shape, 1) < 64


def swap_halves(v):
    return pltpu.roll(v, 64, 1)


def one_hot(mask):
    return jnp.where(mask, 1.0, 0.0).astype(BF16)


def farthest_first(n):
    return sorted(range(1, n), key=lambda d: -min(d, n - d))


def nearest_first(n):
    return sorted(range(1, n), key=lambda d: min(d, n - d))


def finish(scale, rows, inverse, transfer, coefficients):
    out = dot(rows[:, 0:64], inverse[:, 0:64], CONTRACT_LAST, lax.Precision.HIGHEST)
    transfer[...] = out[0:8] * scale
    coefficients[...] = out[8:12]


def kernel(sizes, blocks, basis_b_in, basis_a_in, sketch_in, rows_out, inverse_out, *scratch):
    X, Y, Z = sizes
    ZC = Z * 2
    ZL = Z // 2
    chips = Y * Z
    FX = chips * 8
    FC = FX // Y
    RC = FC * 8
    (block_in, wide_n, by_a, packed, n_in, n_x, s_own, s_zc, s_y, s_all, t_out, t_in, sp_out, sp_in, z_out, z_in,
     mz, s_full, m_to, m_from, gram_out, gram_in, y_out, y_in, basis_bt, basis_at, sketch,
     in_sem, small_sem, s_a, r_a, s_b, r_b, s_n, r_n, s_t, r_t, s_z1, r_z1, s_y1, r_y1, s_z2, r_z2, s_x1, r_x1,
     s_g, r_g, s_y1z, r_y1z) = scratch

    wide = lax.axis_index("wide")
    x = lax.axis_index("pair")
    core = wide % 2
    chip = wide // 2
    z = chip % Z
    y = chip // Z

    def at(dx=0, dy=0, dz=0, dc=0):
        row = ((y + dy) % Y) * Z + (z + dz) % Z
        return (row * 2 + (core + dc) % 2, (x + dx) % X)

    waits = []
    slow_waits = []

    def send(src, dst, ssem, rsem, peer, slow=False):
        copy = pltpu.make_async_remote_copy(
            src_ref=src, dst_ref=dst, send_sem=ssem, recv_sem=rsem, device_id=peer, device_id_type=MESH
        )
        copy.start()
        (slow_waits if slow else waits).append(copy)
        return copy

    def receive(copies):
        for copy in reversed(copies):
            copy.wait_recv()

    def drain(keep=0):
        done = waits[: len(waits) - keep]
        for copy in done:
            copy.wait_send()
        del waits[: len(done)]

    far_z, far_y, far_x = farthest_first(Z), farthest_first(Y), farthest_first(X)
    zc_peers = [(dc, dz) for dz in far_z + [0] for dc in range(2) if dc or dz]
    yc_peers = [(dc, dy) for dy in far_y + [0] for dc in range(2) if dc or dy]
    xc_peers = [(dc, dx) for dx in far_x + [0] for dc in range(2) if dc or dx]

    small = [
        pltpu.make_async_copy(src, dst, small_sem.at[i])
        for i, (src, dst) in enumerate(((sketch_in, sketch), (basis_b_in, basis_bt), (basis_a_in, basis_at)))
    ]
    small[0].start()
    barrier = pltpu.get_barrier_semaphore()
    met = 0
    for dc, dz in zc_peers:
        pl.semaphore_signal(barrier, inc=1, device_id=at(dz=dz, dc=dc), device_id_type=MESH)
        met += 1
    for dc, dy in yc_peers:
        if dy:
            pl.semaphore_signal(barrier, inc=1, device_id=at(dy=dy, dc=dc), device_id_type=MESH)
            met += 1
    for dc, dx in xc_peers:
        if dx:
            pl.semaphore_signal(barrier, inc=1, device_id=at(dx=dx, dc=dc), device_id_type=MESH)
            met += 1

    for load in small[1:]:
        load.start()
    loads = [
        pltpu.make_async_copy(blocks.at[pl.ds(i * RC, RC)], block_in.at[i], in_sem.at[i]) for i in range(Y)
    ]
    for load in loads:
        load.start()

    twice = one_hot(iota((64, 128), 1) % 64 == iota((64, 128), 0))
    small[0].wait()
    s_mine = dot(sketch[...], twice)
    s_own[...] = s_mine
    zc = z * 2 + core
    s_zc[zc] = s_mine
    small[1].wait()
    basis2 = jnp.concatenate([basis_bt[...], basis_bt[...]], axis=0)

    def narrow(i, carry):
        pltpu.make_async_copy(blocks.at[pl.ds(i * RC, RC)], block_in.at[i], in_sem.at[i]).wait()
        wide_n[...] = dot(block_in[i], basis2, CONTRACT_LAST)
        low = low_half((FC, 128))
        odd = (iota((FC, 128), 1) // 32) % 2 == 1
        for t in range(2):
            part = [wide_n[pl.ds(t * 4 + q, FC, stride=8), :] for q in range(4)]
            first = jnp.where(low, part[0], part[2])
            second = jnp.where(low, part[1], part[3])
            lanes = slice(t * 128, t * 128 + 128)
            by_a[0, i, :, lanes] = jnp.where(odd, pltpu.roll(second, 32, 1), first).astype(BF16)
            by_a[1, i, :, lanes] = jnp.where(odd, second, pltpu.roll(first, 96, 1)).astype(BF16)
        return carry

    pl.semaphore_wait(barrier, met)

    got_a = [
        send(s_own, s_zc.at[zc], s_a.at[dc, dz], r_a.at[dc, dz], at(dz=dz, dc=dc)) for dc, dz in zc_peers
    ]

    lax.fori_loop(0, Y, narrow, 0)

    receive(got_a)
    half = ZC // 2
    lo = jnp.concatenate([s_zc[i] for i in range(half)], axis=0)
    hi = jnp.concatenate([s_zc[half + i] for i in range(half)], axis=0)
    rows_h = half * 4
    s_y[y] = jnp.where(low_half((rows_h, 128)), lo, hi).astype(BF16)
    got_b = [send(s_y.at[y], s_y.at[y], s_b.at[dy], r_b.at[dy], at(dy=dy)) for dy in far_y]

    partner = at(dc=1)
    small[2].wait()

    lane_in = iota((256, 256), 0)
    move = one_hot(iota((256, 256), 1) == (lane_in // 8 % 4) * 64 + lane_in // 32 * 8 + lane_in % 8)
    for cc in range(2):
        packed[cc] = dot(by_a[cc].reshape(FX, 256), move).astype(BF16).reshape(Y, FC, 256)

    ZA = Z * 16
    a_part = basis_at[:, pl.ds(pl.multiple_of(y * ZA, ZA), ZA)]
    MR = chips * 4

    def chip_of(index):
        zy = index // 4
        return (zy % Y) * Z + zy // Y

    col = iota((ZA, 256), 1)
    pick = iota((ZA, 256), 0) == (
        z * 16 + ((core + (col // 32) % 2) % 2) * 8 + ((col // 8) % 4) * 2 + (col // 64) % 2
    )
    a_cols = dot(a_part, one_hot(pick)).astype(BF16)
    spread = one_hot(chip_of(iota((MR, chips), 0)) == iota((MR, chips), 1))
    rows_a = dot(spread, a_cols)
    for rh in range(2):
        keep = iota((MR, 256), 1) % 8 == rh * 4 + iota((MR, 256), 0) % 4
        m_to[rh] = jnp.where(keep, rows_a, 0.0).astype(BF16)

    receive(got_b)
    low = low_half((rows_h, 128))
    for i in range(Y):
        v = s_y[i].astype(F32)
        w = swap_halves(v)
        s_all[2 * i * rows_h : (2 * i + 1) * rows_h, :] = jnp.where(low, v, w).astype(BF16)
        s_all[(2 * i + 1) * rows_h : (2 * i + 2) * rows_h, :] = jnp.where(low, w, v).astype(BF16)

    low = low_half((8, 128))
    for cc in range(2):
        t = dot(packed[cc].reshape(FX, 256), s_all[...], CONTRACT_FIRST)
        for xx in range(4):
            for ah in range(4):
                at_a = xx * 64 + ah * 16
                t_out[cc, xx, ah] = jnp.where(low, t[at_a : at_a + 8], t[at_a + 8 : at_a + 16])
    got_t = [
        send(
            t_out.at[(core + dc) % 2, (x + dx) % X],
            t_in.at[dc, dx],
            s_t.at[dc, dx],
            r_t.at[dc, dx],
            at(dx=dx, dc=dc),
        )
        for dc, dx in xc_peers
    ]
    def spread_fibres(peers):
        return [
            send(
                packed.at[(core + dc) % 2, (y + dy) % Y],
                n_in.at[dc, dy],
                s_n.at[dc, dy],
                r_n.at[dc, dy],
                at(dy=dy, dc=dc),
                slow=True,
            )
            for dc, dy in peers
        ]

    got_n = spread_fibres([p for p in yc_peers if p[0] == 0])
    mine = t_out[core, x]
    other = None
    drain(len(got_t))
    for (dc, dx), copy in reversed(list(zip(xc_peers, got_t))):
        copy.wait_recv()
        if dc == 0:
            mine = mine + t_in[0, dx]
        else:
            other = t_in[1, dx] if other is None else other + t_in[1, dx]
    u = jnp.concatenate([mine.reshape(32, 128), other.reshape(32, 128)], axis=0)
    low = low_half((64, 128))
    v = swap_halves(u)
    u = jnp.concatenate([jnp.where(low, u, v), jnp.where(low, v, u)], axis=0)
    top = u.astype(BF16)
    rest = (u - top.astype(F32)).astype(BF16)
    u = jnp.concatenate([top, rest], axis=0)
    low = low_half((MR, 128))
    part = jnp.where(low, dot(m_to[0], u), dot(m_to[1], u))
    RZ = Y * 4
    for i in range(Z):
        sp_out[i] = part[i * RZ : (i + 1) * RZ].astype(BF16)

    got = [
        send(sp_out.at[(z + dz) % Z], sp_in.at[dz], s_z1.at[dz], r_z1.at[dz], at(dz=dz)) for dz in far_z
    ]
    total = sp_out[z].astype(F32)
    drain(len(got))

    row = iota((128, ZA), 0)
    pick = one_hot(iota((128, ZA), 1) == z * 16 + ((core + row // 64) % 2) * 8 + (row // 8) % 8)
    spread = one_hot(chip_of(iota((chips, MR), 1)) == iota((chips, MR), 0))
    for dy in range(Y):
        a_part = basis_at[:, pl.ds(pl.multiple_of(((y + Y - dy) % Y) * ZA, ZA), ZA)]
        cols_a = dot(dot(pick, a_part, CONTRACT_LAST).astype(BF16), spread)
        for rh in range(2):
            keep = iota((128, MR), 0) % 8 == rh * 4 + iota((128, MR), 1) % 4
            m_from[dy * 128 : dy * 128 + 128, rh * MR : (rh + 1) * MR] = jnp.where(keep, cols_a, 0.0).astype(BF16)

    for dz, copy in reversed(list(zip(far_z, got))):
        copy.wait_recv()
        total = total + sp_in[dz].astype(F32)
    z_out[...] = total.astype(BF16)
    got = [send(z_out, z_in.at[dy], s_y1.at[dy], r_y1.at[dy], at(dy=dy)) for dy in far_y]
    drain(len(got))
    for dy, copy in reversed(list(zip(far_y, got))):
        copy.wait_recv()
        total = total + z_in[dy].astype(F32)
    for i in range(Y):
        mz[i] = total[i * 4 : i * 4 + 4]
    s_full[x, z] = total.astype(BF16)
    spot = s_full.at[x, z]
    got = {dz: send(spot, spot, s_z2.at[dz], r_z2.at[dz], at(dz=dz)) for dz in far_z}
    got_n += spread_fibres([p for p in yc_peers if p[0] == 1])
    got_x = []
    drain(len(got))
    for dz in [0] + nearest_first(Z):
        if dz:
            receive([got[dz]])
        spot = s_full.at[x, (z + Z - dz) % Z]
        for dx in far_x:
            got_x.append(send(spot, spot, s_x1.at[dx, dz], r_x1.at[dx, dz], at(dx=dx)))
    drain(len(got_x))

    receive(got_n)
    half = low_half((FC, 128))
    for dy in range(Y):
        own = (n_in[0, dy] if dy else packed[core, y]).astype(F32)
        other = n_in[1, dy].astype(F32)
        spot = slice(dy * 128, dy * 128 + 128)
        for xp in range(X // 2):
            a_side = own[:, xp * 128 : xp * 128 + 128]
            b_side = other[:, xp * 128 : xp * 128 + 128]
            n_x[2 * xp, :, spot] = jnp.where(half, a_side, swap_halves(b_side)).astype(BF16)
            n_x[2 * xp + 1, :, spot] = jnp.where(half, swap_halves(a_side), b_side).astype(BF16)
    for i in range(0, len(got_x), len(far_x)):
        receive(got_x[i : i + len(far_x)])
    s_x = [s_full[i].reshape(MR, 128) for i in range(X)]

    big = dot(s_x[0], s_x[0], CONTRACT_FIRST)
    for i in range(1, X):
        big = big + dot(s_x[i], s_x[i], CONTRACT_FIRST)
    gram_out[...] = swap_halves(big[0:64]) + big[64:128]
    got_g = send(gram_out, gram_in, s_g, r_g, partner)

    low = low_half((MR, 128))
    rhs = []
    for xp in range(X // 2):
        s0 = s_x[2 * xp].astype(F32)
        s1 = s_x[2 * xp + 1].astype(F32)
        rhs.append(
            jnp.concatenate(
                [jnp.where(low, s0, swap_halves(s1)), jnp.where(low, swap_halves(s0), s1)], axis=0
            ).astype(BF16)
        )
    w_rows = dot(m_from[...], jnp.concatenate(rhs, axis=1)).astype(BF16)
    by_x = dot(n_x[...].reshape(X * FC, Y * 128), w_rows)
    even = by_x[0:FC, 0:128]
    odd = by_x[FC : 2 * FC, 0:128]
    for xp in range(1, X // 2):
        even = even + by_x[2 * xp * FC : (2 * xp + 1) * FC, xp * 128 : xp * 128 + 128]
        odd = odd + by_x[(2 * xp + 1) * FC : (2 * xp + 2) * FC, xp * 128 : xp * 128 + 128]
    ypart = jnp.where(half, even + swap_halves(odd), swap_halves(even) + odd)
    ypart = jnp.where(low_half((FC // 2, 128)), ypart[0 : FC // 2], ypart[FC // 2 : FC])
    for i in range(ZL):
        for cc in range(2):
            y_out[i, cc] = ypart[i * 8 + cc * 4 : i * 8 + cc * 4 + 4]
    got_y = [
        send(
            y_out.at[((z + dz) % Z) % ZL, (core + dc) % 2],
            y_in.at[dc, dz],
            s_y1z.at[dc, dz],
            r_y1z.at[dc, dz],
            at(dz=dz, dc=dc),
        )
        for dc, dz in zc_peers
    ]

    receive([got_g])
    g = gram_out[...] + gram_in[...]
    low = low_half((64, 128))
    g = jnp.where(low, jnp.where(iota((64, 128), 0) == iota((64, 128), 1), 1.0, 0.0), g)
    tiles = [g[i * 8 : i * 8 + 8] for i in range(8)]
    sub = iota((8, 128), 0)

    def lane(v, j):
        return jnp.broadcast_to(v[:, 64 + j : 65 + j], v.shape)

    def eliminate(tiles, first, last):
        for j in range(first, last, 4):
            home, pos = j // 8, j % 8
            lines = [tiles[home][pos + t : pos + t + 1] for t in range(4)]
            u = [[lane(lines[t], j + v) for v in range(4)] for t in range(4)]
            inv = []
            for t in range(4):
                inv.append(1.0 / u[t][t])
                for v in range(t + 1, 4):
                    ratio = u[t][v] * inv[t]
                    for w in range(v, 4):
                        u[v][w] = u[v][w] - ratio * u[t][w]
                    lines[v] = lines[v] - ratio * lines[t]
            for i in range(home, 8):
                c = [lane(tiles[i], j + v) for v in range(4)]
                new = tiles[i]
                for t in range(4):
                    m = c[t] * inv[t]
                    if i == home:
                        m = jnp.where(sub > pos + t, m, 0.0)
                    for v in range(t + 1, 4):
                        c[v] = c[v] - m * u[t][v]
                    new = new - m * lines[t]
                tiles[i] = new
        return tiles

    tiles = eliminate(tiles, 0, 64)
    elim = jnp.concatenate(tiles, axis=0)
    diagonal = jnp.where(iota((64, 128), 1) == iota((64, 128), 0) + 64, elim, 0.0)
    pivots = jnp.sum(diagonal, axis=1, keepdims=True)
    inverse_out[...] = elim * (1.0 / jnp.sqrt(pivots))

    drain()
    for copy in slow_waits:
        copy.wait_send()
    acc = y_out[z % ZL, core]
    for (dc, dz), copy in reversed(list(zip(zc_peers, got_y))):
        copy.wait_recv()
        acc = acc + y_in[dc, dz]
    acc = jnp.where(z // ZL == 0, acc, swap_halves(acc))
    s_mine = mz[y]
    rows_out[...] = jnp.concatenate([s_mine, swap_halves(s_mine), acc, acc], axis=0)


def scratch_for(sizes, cb):
    X, Y, Z = sizes
    ZC = Z * 2
    ZL = Z // 2
    chips = Y * Z
    FX = chips * 8
    FC = FX // Y
    MR = chips * 4
    RZ = Y * 4
    dma = pltpu.SemaphoreType.DMA
    return [
        pltpu.VMEM((Y, FC * 8, cb), BF16),
        pltpu.VMEM((FC * 8, 128), F32),
        pltpu.VMEM((2, Y, FC, 256), BF16),
        pltpu.VMEM((2, Y, FC, 256), BF16),
        pltpu.VMEM((2, Y, FC, 256), BF16),
        pltpu.VMEM((X, FC, Y * 128), BF16),
        pltpu.VMEM((4, 128), F32),
        pltpu.VMEM((ZC, 4, 128), F32),
        pltpu.VMEM((Y, ZC * 2, 128), BF16),
        pltpu.VMEM((FX, 128), BF16),
        pltpu.VMEM((2, 4, 4, 8, 128), F32),
        pltpu.VMEM((2, X, 4, 8, 128), F32),
        pltpu.VMEM((Z, RZ, 128), BF16),
        pltpu.VMEM((Z, RZ, 128), BF16),
        pltpu.VMEM((RZ, 128), BF16),
        pltpu.VMEM((Y, RZ, 128), BF16),
        pltpu.VMEM((Y, 4, 128), F32),
        pltpu.VMEM((X, Z, RZ, 128), BF16),
        pltpu.VMEM((2, MR, 256), BF16),
        pltpu.VMEM((Y * 128, 2 * MR), BF16),
        pltpu.VMEM((64, 128), F32),
        pltpu.VMEM((64, 128), F32),
        pltpu.VMEM((ZL, 2, 4, 128), F32),
        pltpu.VMEM((2, Z, 4, 128), F32),
        pltpu.VMEM((64, cb), BF16),
        pltpu.VMEM((chips, chips * 16), BF16),
        pltpu.VMEM((4, 64), BF16),
        dma((Y,)),
        dma((3,)),
        dma((2, Z)), dma((2, Z)),
        dma((Y,)), dma((Y,)),
        dma((2, Y)), dma((2, Y)),
        dma((2, X)), dma((2, X)),
        dma((Z,)), dma((Z,)),
        dma((Y,)), dma((Y,)),
        dma((Z,)), dma((Z,)),
        dma((X, Z)), dma((X, Z)),
        dma, dma,
        dma((2, Z)), dma((2, Z)),
    ]


def per_device(sizes, blocks, basis_a, basis_b, sketch):
    fibres, own_a, cb = blocks.shape
    vmem = pl.BlockSpec(memory_space=pltpu.VMEM)
    anywhere = pl.BlockSpec(memory_space=pl.ANY)
    rows, inverse = pl.pallas_call(
        functools.partial(kernel, sizes),
        out_shape=(jax.ShapeDtypeStruct((16, 128), F32), jax.ShapeDtypeStruct((64, 128), F32)),
        in_specs=[anywhere] * 4,
        out_specs=(vmem, vmem),
        scratch_shapes=scratch_for(sizes, cb),
        compiler_params=pltpu.CompilerParams(collective_id=0, has_side_effects=True),
        name="tucker",
    )(blocks.reshape(fibres * own_a, cb), basis_b.T, basis_a.T, sketch)
    chips = sizes[1] * sizes[2]
    return pl.pallas_call(
        functools.partial(finish, float((chips * 64) ** 0.5)),
        out_shape=(jax.ShapeDtypeStruct((8, 64), F32), jax.ShapeDtypeStruct((4, 64), F32)),
        in_specs=[vmem, vmem],
        out_specs=(vmem, vmem),
        name="finish",
    )(rows, inverse)


def solution(mesh):
    chips = mesh.shape["wide"] // 2
    side = int(round(chips ** 0.5))
    sizes = (mesh.shape["pair"], side, chips // side)
    placed = (P("pair", "wide", None), P(), P(), P(("pair", "wide"), None))
    return jax.shard_map(
        functools.partial(per_device, sizes),
        mesh=mesh,
        in_specs=placed,
        out_specs=(P(("wide", "pair"), None), P(("pair", "wide"), None)),
        check_vma=False,
    )
```

```python
import functools

import jax
import jax.numpy as jnp
from jax import lax
from jax.experimental import pallas as pl
from jax.experimental.pallas import tpu as pltpu
from jax.sharding import PartitionSpec as P

MESH = pl.DeviceIdType.MESH
F32 = jnp.float32
BF16 = jnp.bfloat16
CONTRACT_LAST = (((1,), (1,)), ((), ()))
CONTRACT_FIRST = (((0,), (0,)), ((), ()))


def iota(shape, dim):
    return lax.broadcasted_iota(jnp.int32, shape, dim)


def dot(a, b, dims=(((1,), (0,)), ((), ())), precision=None):
    return lax.dot_general(a, b, dims, preferred_element_type=F32, precision=precision)


def low_half(shape):
    return iota(shape, 1) < 64


def swap_halves(v):
    return pltpu.roll(v, 64, 1)


def one_hot(mask):
    return jnp.where(mask, 1.0, 0.0).astype(BF16)


def farthest_first(n):
    return sorted(range(1, n), key=lambda d: -min(d, n - d))


def nearest_first(n):
    return sorted(range(1, n), key=lambda d: min(d, n - d))


def finish(scale, rows, inverse, transfer, coefficients):
    out = dot(rows[:, 0:64], inverse[:, 0:64], CONTRACT_LAST, lax.Precision.HIGHEST)
    transfer[...] = out[0:8] * scale
    coefficients[...] = out[8:12]


def kernel(sizes, blocks, basis_b_in, basis_a_in, sketch_in, rows_out, inverse_out, *scratch):
    X, Y, Z = sizes
    ZC = Z * 2
    ZL = Z // 2
    chips = Y * Z
    FX = chips * 8
    FC = FX // Y
    RC = FC * 8
    (block_in, wide_n, by_a, packed, n_in, n_x, s_own, s_zc, s_y, s_all, t_out, t_in, sp_out, sp_in, z_out, z_in,
     mz, s_full, m_to, m_from, gram_out, gram_in, y_out, y_in, basis_bt, basis_at, sketch,
     in_sem, small_sem, s_a, r_a, s_b, r_b, s_n, r_n, s_t, r_t, s_z1, r_z1, s_y1, r_y1, s_z2, r_z2, s_x1, r_x1,
     s_g, r_g, s_y1z, r_y1z) = scratch

    wide = lax.axis_index("wide")
    x = lax.axis_index("pair")
    core = wide % 2
    chip = wide // 2
    z = chip % Z
    y = chip // Z

    def at(dx=0, dy=0, dz=0, dc=0):
        row = ((y + dy) % Y) * Z + (z + dz) % Z
        return (row * 2 + (core + dc) % 2, (x + dx) % X)

    def send(src, dst, ssem, rsem, peer):
        copy = pltpu.make_async_remote_copy(
            src_ref=src, dst_ref=dst, send_sem=ssem, recv_sem=rsem, device_id=peer, device_id_type=MESH
        )
        copy.start()
        return copy

    def all_of(space, ssem, rsem):
        return pltpu.make_async_remote_copy(
            src_ref=space, dst_ref=space, send_sem=ssem, recv_sem=rsem, device_id=at(dc=1), device_id_type=MESH
        )

    far_z, far_y, far_x = farthest_first(Z), farthest_first(Y), farthest_first(X)
    zc_peers = [(dc, dz) for dz in far_z + [0] for dc in range(2) if dc or dz]
    yc_peers = [(dc, dy) for dy in far_y + [0] for dc in range(2) if dc or dy]
    xc_peers = [(dc, dx) for dx in far_x + [0] for dc in range(2) if dc or dx]

    small = [
        pltpu.make_async_copy(src, dst, small_sem.at[i])
        for i, (src, dst) in enumerate(((sketch_in, sketch), (basis_b_in, basis_bt), (basis_a_in, basis_at)))
    ]
    small[0].start()
    barrier = pltpu.get_barrier_semaphore()
    met = 0
    for dc, dz in zc_peers:
        pl.semaphore_signal(barrier, inc=1, device_id=at(dz=dz, dc=dc), device_id_type=MESH)
        met += 1
    for dc, dy in yc_peers:
        if dy:
            pl.semaphore_signal(barrier, inc=1, device_id=at(dy=dy, dc=dc), device_id_type=MESH)
            met += 1
    for dc, dx in xc_peers:
        if dx:
            pl.semaphore_signal(barrier, inc=1, device_id=at(dx=dx, dc=dc), device_id_type=MESH)
            met += 1

    for load in small[1:]:
        load.start()
    loads = [
        pltpu.make_async_copy(blocks.at[pl.ds(i * RC, RC)], block_in.at[i], in_sem.at[i]) for i in range(Y)
    ]
    for load in loads:
        load.start()

    twice = one_hot(iota((64, 128), 1) % 64 == iota((64, 128), 0))
    small[0].wait()
    s_mine = dot(sketch[...], twice)
    s_own[...] = s_mine
    zc = z * 2 + core
    s_zc[zc] = s_mine
    small[1].wait()
    basis2 = jnp.concatenate([basis_bt[...], basis_bt[...]], axis=0)

    def narrow(i, carry):
        pltpu.make_async_copy(blocks.at[pl.ds(i * RC, RC)], block_in.at[i], in_sem.at[i]).wait()
        wide_n[...] = dot(block_in[i], basis2, CONTRACT_LAST)
        low = low_half((FC, 128))
        odd = (iota((FC, 128), 1) // 32) % 2 == 1
        for t in range(2):
            part = [wide_n[pl.ds(t * 4 + q, FC, stride=8), :] for q in range(4)]
            first = jnp.where(low, part[0], part[2])
            second = jnp.where(low, part[1], part[3])
            lanes = slice(t * 128, t * 128 + 128)
            by_a[0, i, :, lanes] = jnp.where(odd, pltpu.roll(second, 32, 1), first).astype(BF16)
            by_a[1, i, :, lanes] = jnp.where(odd, second, pltpu.roll(first, 96, 1)).astype(BF16)
        return carry

    pl.semaphore_wait(barrier, met)

    for dc, dz in zc_peers:
        send(s_own, s_zc.at[zc], s_a, r_a, at(dz=dz, dc=dc))
    got_a = all_of(s_zc.at[pl.ds(1, ZC - 1)], s_a, r_a)

    lax.fori_loop(0, Y, narrow, 0)

    got_a.wait_recv()
    half = ZC // 2
    lo = jnp.concatenate([s_zc[i] for i in range(half)], axis=0)
    hi = jnp.concatenate([s_zc[half + i] for i in range(half)], axis=0)
    rows_h = half * 4
    s_y[y] = jnp.where(low_half((rows_h, 128)), lo, hi).astype(BF16)
    for dy in far_y:
        send(s_y.at[y], s_y.at[y], s_b, r_b, at(dy=dy))
    got_b = all_of(s_y.at[pl.ds(1, Y - 1)], s_b, r_b)

    partner = at(dc=1)
    small[2].wait()

    lane_in = iota((256, 256), 0)
    move = one_hot(iota((256, 256), 1) == (lane_in // 8 % 4) * 64 + lane_in // 32 * 8 + lane_in % 8)
    for cc in range(2):
        packed[cc] = dot(by_a[cc].reshape(FX, 256), move).astype(BF16).reshape(Y, FC, 256)

    ZA = Z * 16
    a_part = basis_at[:, pl.ds(pl.multiple_of(y * ZA, ZA), ZA)]
    MR = chips * 4

    def chip_of(index):
        zy = index // 4
        return (zy % Y) * Z + zy // Y

    col = iota((ZA, 256), 1)
    pick = iota((ZA, 256), 0) == (
        z * 16 + ((core + (col // 32) % 2) % 2) * 8 + ((col // 8) % 4) * 2 + (col // 64) % 2
    )
    a_cols = dot(a_part, one_hot(pick)).astype(BF16)
    spread = one_hot(chip_of(iota((MR, chips), 0)) == iota((MR, chips), 1))
    rows_a = dot(spread, a_cols)
    for rh in range(2):
        keep = iota((MR, 256), 1) % 8 == rh * 4 + iota((MR, 256), 0) % 4
        m_to[rh] = jnp.where(keep, rows_a, 0.0).astype(BF16)

    got_b.wait_recv()
    low = low_half((rows_h, 128))
    for i in range(Y):
        v = s_y[i].astype(F32)
        w = swap_halves(v)
        s_all[2 * i * rows_h : (2 * i + 1) * rows_h, :] = jnp.where(low, v, w).astype(BF16)
        s_all[(2 * i + 1) * rows_h : (2 * i + 2) * rows_h, :] = jnp.where(low, w, v).astype(BF16)

    low = low_half((8, 128))
    for cc in range(2):
        t = dot(packed[cc].reshape(FX, 256), s_all[...], CONTRACT_FIRST)
        for xx in range(4):
            for ah in range(4):
                at_a = xx * 64 + ah * 16
                t_out[cc, xx, ah] = jnp.where(low, t[at_a : at_a + 8], t[at_a + 8 : at_a + 16])
    for dc, dx in xc_peers:
        send(t_out.at[(core + dc) % 2, (x + dx) % X], t_in.at[dc * X + dx], s_t, r_t, at(dx=dx, dc=dc))
    got_t = all_of(t_in.at[pl.ds(1, 2 * X - 1)], s_t, r_t)

    def spread_fibres(peers):
        for dc, dy in peers:
            send(packed.at[(core + dc) % 2, (y + dy) % Y], n_in.at[dc * Y + dy], s_n, r_n, at(dy=dy, dc=dc))

    spread_fibres([p for p in yc_peers if p[0] == 0])
    mine = t_out[core, x]
    for copy in (got_a, got_b):
        copy.wait_send()
    got_t.wait_recv()
    for dx in range(1, X):
        mine = mine + t_in[dx]
    other = t_in[X]
    for dx in range(1, X):
        other = other + t_in[X + dx]
    u = jnp.concatenate([mine.reshape(32, 128), other.reshape(32, 128)], axis=0)
    low = low_half((64, 128))
    v = swap_halves(u)
    u = jnp.concatenate([jnp.where(low, u, v), jnp.where(low, v, u)], axis=0)
    top = u.astype(BF16)
    rest = (u - top.astype(F32)).astype(BF16)
    u = jnp.concatenate([top, rest], axis=0)
    low = low_half((MR, 128))
    part = jnp.where(low, dot(m_to[0], u), dot(m_to[1], u))
    RZ = Y * 4
    for i in range(Z):
        sp_out[i] = part[i * RZ : (i + 1) * RZ].astype(BF16)

    for dz in far_z:
        send(sp_out.at[(z + dz) % Z], sp_in.at[dz], s_z1, r_z1, at(dz=dz))
    got_z = all_of(sp_in.at[pl.ds(1, Z - 1)], s_z1, r_z1)
    total = sp_out[z].astype(F32)
    got_t.wait_send()

    row = iota((128, ZA), 0)
    pick = one_hot(iota((128, ZA), 1) == z * 16 + ((core + row // 64) % 2) * 8 + (row // 8) % 8)
    spread = one_hot(chip_of(iota((chips, MR), 1)) == iota((chips, MR), 0))
    for dy in range(Y):
        a_part = basis_at[:, pl.ds(pl.multiple_of(((y + Y - dy) % Y) * ZA, ZA), ZA)]
        cols_a = dot(dot(pick, a_part, CONTRACT_LAST).astype(BF16), spread)
        for rh in range(2):
            keep = iota((128, MR), 0) % 8 == rh * 4 + iota((128, MR), 1) % 4
            m_from[dy * 128 : dy * 128 + 128, rh * MR : (rh + 1) * MR] = jnp.where(keep, cols_a, 0.0).astype(BF16)

    got_z.wait_recv()
    for dz in range(1, Z):
        total = total + sp_in[dz].astype(F32)
    z_out[...] = total.astype(BF16)
    for dy in far_y:
        send(z_out, z_in.at[dy], s_y1, r_y1, at(dy=dy))
    got_r = all_of(z_in.at[pl.ds(1, Y - 1)], s_y1, r_y1)
    got_z.wait_send()
    got_r.wait_recv()
    for dy in range(1, Y):
        total = total + z_in[dy].astype(F32)
    for i in range(Y):
        mz[i] = total[i * 4 : i * 4 + 4]
    s_full[x, z] = total.astype(BF16)
    spot = s_full.at[x, z]
    got = {dz: send(spot, spot, s_z2, r_z2.at[dz], at(dz=dz)) for dz in far_z}
    spread_fibres([p for p in yc_peers if p[0] == 1])
    got_n = all_of(n_in.at[pl.ds(1, 2 * Y - 1)], s_n, r_n)
    got_r.wait_send()
    for dz in [0] + nearest_first(Z):
        if dz:
            got[dz].wait_recv()
        spot = s_full.at[x, (z + Z - dz) % Z]
        for dx in far_x:
            send(spot, spot, s_x1.at[dx], r_x1.at[dx], at(dx=dx))
    got_x = [all_of(s_full.at[(x + X - dx) % X], s_x1.at[dx], r_x1.at[dx]) for dx in nearest_first(X)]
    all_of(sp_in.at[pl.ds(1, Z - 1)], s_z2, r_z2.at[0]).wait_send()

    got_n.wait_recv()
    half = low_half((FC, 128))
    for dy in range(Y):
        own = (n_in[dy] if dy else packed[core, y]).astype(F32)
        other = n_in[Y + dy].astype(F32)
        spot = slice(dy * 128, dy * 128 + 128)
        for xp in range(X // 2):
            a_side = own[:, xp * 128 : xp * 128 + 128]
            b_side = other[:, xp * 128 : xp * 128 + 128]
            n_x[2 * xp, :, spot] = jnp.where(half, a_side, swap_halves(b_side)).astype(BF16)
            n_x[2 * xp + 1, :, spot] = jnp.where(half, swap_halves(a_side), b_side).astype(BF16)
    for copy in got_x:
        copy.wait_recv()
    s_x = [s_full[i].reshape(MR, 128) for i in range(X)]

    big = dot(s_x[0], s_x[0], CONTRACT_FIRST)
    for i in range(1, X):
        big = big + dot(s_x[i], s_x[i], CONTRACT_FIRST)
    gram_out[...] = swap_halves(big[0:64]) + big[64:128]
    got_g = send(gram_out, gram_in, s_g, r_g, partner)

    low = low_half((MR, 128))
    rhs = []
    for xp in range(X // 2):
        s0 = s_x[2 * xp].astype(F32)
        s1 = s_x[2 * xp + 1].astype(F32)
        rhs.append(
            jnp.concatenate(
                [jnp.where(low, s0, swap_halves(s1)), jnp.where(low, swap_halves(s0), s1)], axis=0
            ).astype(BF16)
        )
    w_rows = dot(m_from[...], jnp.concatenate(rhs, axis=1)).astype(BF16)
    by_x = dot(n_x[...].reshape(X * FC, Y * 128), w_rows)
    even = by_x[0:FC, 0:128]
    odd = by_x[FC : 2 * FC, 0:128]
    for xp in range(1, X // 2):
        even = even + by_x[2 * xp * FC : (2 * xp + 1) * FC, xp * 128 : xp * 128 + 128]
        odd = odd + by_x[(2 * xp + 1) * FC : (2 * xp + 2) * FC, xp * 128 : xp * 128 + 128]
    ypart = jnp.where(half, even + swap_halves(odd), swap_halves(even) + odd)
    ypart = jnp.where(low_half((FC // 2, 128)), ypart[0 : FC // 2], ypart[FC // 2 : FC])
    for i in range(ZL):
        for cc in range(2):
            y_out[i, cc] = ypart[i * 8 + cc * 4 : i * 8 + cc * 4 + 4]
    for dc, dz in zc_peers:
        send(y_out.at[((z + dz) % Z) % ZL, (core + dc) % 2], y_in.at[dc * Z + dz], s_y1z, r_y1z, at(dz=dz, dc=dc))
    got_y = all_of(y_in.at[pl.ds(1, 2 * Z - 1)], s_y1z, r_y1z)

    got_g.wait_recv()
    g = gram_out[...] + gram_in[...]
    low = low_half((64, 128))
    g = jnp.where(low, jnp.where(iota((64, 128), 0) == iota((64, 128), 1), 1.0, 0.0), g)
    tiles = [g[i * 8 : i * 8 + 8] for i in range(8)]
    sub = iota((8, 128), 0)

    def lane(v, j):
        return jnp.broadcast_to(v[:, 64 + j : 65 + j], v.shape)

    def eliminate(tiles, first, last):
        for j in range(first, last, 4):
            home, pos = j // 8, j % 8
            lines = [tiles[home][pos + t : pos + t + 1] for t in range(4)]
            u = [[lane(lines[t], j + v) for v in range(4)] for t in range(4)]
            inv = []
            for t in range(4):
                inv.append(1.0 / u[t][t])
                for v in range(t + 1, 4):
                    ratio = u[t][v] * inv[t]
                    for w in range(v, 4):
                        u[v][w] = u[v][w] - ratio * u[t][w]
                    lines[v] = lines[v] - ratio * lines[t]
            for i in range(home, 8):
                c = [lane(tiles[i], j + v) for v in range(4)]
                new = tiles[i]
                for t in range(4):
                    m = c[t] * inv[t]
                    if i == home:
                        m = jnp.where(sub > pos + t, m, 0.0)
                    for v in range(t + 1, 4):
                        c[v] = c[v] - m * u[t][v]
                    new = new - m * lines[t]
                tiles[i] = new
        return tiles

    tiles = eliminate(tiles, 0, 64)
    elim = jnp.concatenate(tiles, axis=0)
    diagonal = jnp.where(iota((64, 128), 1) == iota((64, 128), 0) + 64, elim, 0.0)
    pivots = jnp.sum(diagonal, axis=1, keepdims=True)
    inverse_out[...] = elim * (1.0 / jnp.sqrt(pivots))

    for copy in (got_n, *got_x, got_g, got_y):
        copy.wait_send()
    acc = y_out[z % ZL, core]
    got_y.wait_recv()
    for i in range(1, 2 * Z):
        acc = acc + y_in[i]
    acc = jnp.where(z // ZL == 0, acc, swap_halves(acc))
    s_mine = mz[y]
    rows_out[...] = jnp.concatenate([s_mine, swap_halves(s_mine), acc, acc], axis=0)


def scratch_for(sizes, cb):
    X, Y, Z = sizes
    ZC = Z * 2
    ZL = Z // 2
    chips = Y * Z
    FX = chips * 8
    FC = FX // Y
    MR = chips * 4
    RZ = Y * 4
    dma = pltpu.SemaphoreType.DMA
    return [
        pltpu.VMEM((Y, FC * 8, cb), BF16),
        pltpu.VMEM((FC * 8, 128), F32),
        pltpu.VMEM((2, Y, FC, 256), BF16),
        pltpu.VMEM((2, Y, FC, 256), BF16),
        pltpu.VMEM((2 * Y, FC, 256), BF16),
        pltpu.VMEM((X, FC, Y * 128), BF16),
        pltpu.VMEM((4, 128), F32),
        pltpu.VMEM((ZC, 4, 128), F32),
        pltpu.VMEM((Y, ZC * 2, 128), BF16),
        pltpu.VMEM((FX, 128), BF16),
        pltpu.VMEM((2, 4, 4, 8, 128), F32),
        pltpu.VMEM((2 * X, 4, 8, 128), F32),
        pltpu.VMEM((Z, RZ, 128), BF16),
        pltpu.VMEM((Z, RZ, 128), BF16),
        pltpu.VMEM((RZ, 128), BF16),
        pltpu.VMEM((Y, RZ, 128), BF16),
        pltpu.VMEM((Y, 4, 128), F32),
        pltpu.VMEM((X, Z, RZ, 128), BF16),
        pltpu.VMEM((2, MR, 256), BF16),
        pltpu.VMEM((Y * 128, 2 * MR), BF16),
        pltpu.VMEM((64, 128), F32),
        pltpu.VMEM((64, 128), F32),
        pltpu.VMEM((ZL, 2, 4, 128), F32),
        pltpu.VMEM((2 * Z, 4, 128), F32),
        pltpu.VMEM((64, cb), BF16),
        pltpu.VMEM((chips, chips * 16), BF16),
        pltpu.VMEM((4, 64), BF16),
        dma((Y,)),
        dma((3,)),
        dma, dma,
        dma, dma,
        dma, dma,
        dma, dma,
        dma, dma,
        dma, dma,
        dma, dma((Z,)),
        dma((X,)), dma((X,)),
        dma, dma,
        dma, dma,
    ]


def per_device(sizes, blocks, basis_a, basis_b, sketch):
    fibres, own_a, cb = blocks.shape
    vmem = pl.BlockSpec(memory_space=pltpu.VMEM)
    anywhere = pl.BlockSpec(memory_space=pl.ANY)
    rows, inverse = pl.pallas_call(
        functools.partial(kernel, sizes),
        out_shape=(jax.ShapeDtypeStruct((16, 128), F32), jax.ShapeDtypeStruct((64, 128), F32)),
        in_specs=[anywhere] * 4,
        out_specs=(vmem, vmem),
        scratch_shapes=scratch_for(sizes, cb),
        compiler_params=pltpu.CompilerParams(collective_id=0, has_side_effects=True),
        name="tucker",
    )(blocks.reshape(fibres * own_a, cb), basis_b.T, basis_a.T, sketch)
    chips = sizes[1] * sizes[2]
    return pl.pallas_call(
        functools.partial(finish, float((chips * 64) ** 0.5)),
        out_shape=(jax.ShapeDtypeStruct((8, 64), F32), jax.ShapeDtypeStruct((4, 64), F32)),
        in_specs=[vmem, vmem],
        out_specs=(vmem, vmem),
        name="finish",
    )(rows, inverse)


def solution(mesh):
    chips = mesh.shape["wide"] // 2
    side = int(round(chips ** 0.5))
    sizes = (mesh.shape["pair"], side, chips // side)
    placed = (P("pair", "wide", None), P(), P(), P(("pair", "wide"), None))
    return jax.shard_map(
        functools.partial(per_device, sizes),
        mesh=mesh,
        in_specs=placed,
        out_specs=(P(("wide", "pair"), None), P(("pair", "wide"), None)),
        check_vma=False,
    )
```

```python
import functools

import jax
import jax.numpy as jnp
from jax import lax
from jax.experimental import pallas as pl
from jax.experimental.pallas import tpu as pltpu
from jax.sharding import PartitionSpec as P

MESH = pl.DeviceIdType.MESH
F32 = jnp.float32
BF16 = jnp.bfloat16
CONTRACT_LAST = (((1,), (1,)), ((), ()))
CONTRACT_FIRST = (((0,), (0,)), ((), ()))


def iota(shape, dim):
    return lax.broadcasted_iota(jnp.int32, shape, dim)


def dot(a, b, dims=(((1,), (0,)), ((), ())), precision=None):
    return lax.dot_general(a, b, dims, preferred_element_type=F32, precision=precision)


def low_half(shape):
    return iota(shape, 1) < 64


def swap_halves(v):
    return pltpu.roll(v, 64, 1)


def one_hot(mask):
    return jnp.where(mask, 1.0, 0.0).astype(BF16)


def farthest_first(n):
    return sorted(range(1, n), key=lambda d: -min(d, n - d))


def nearest_first(n):
    return sorted(range(1, n), key=lambda d: min(d, n - d))


def finish(rows, transfer, coefficients):
    transfer[...] = rows[0:8, 0:64]
    coefficients[...] = rows[8:12, 0:64]


def kernel(sizes, blocks, basis_b_in, basis_a_in, sketch_in, rows_out, *scratch):
    X, Y, Z = sizes
    ZC = Z * 2
    ZL = Z // 2
    chips = Y * Z
    FX = chips * 8
    FC = FX // Y
    RC = FC * 8
    (block_in, wide_n, by_a, packed, n_in, n_x, s_own, s_zc, s_y, s_all, t_out, t_in, sp_out, sp_in, z_out, z_in,
     mz, s_full, m_to, m_from, gram_out, gram_in, y_out, y_in, basis_bt, basis_at, sketch,
     in_sem, small_sem, s_a, r_a, s_b, r_b, s_n, r_n, s_t, r_t, s_z1, r_z1, s_y1, r_y1, s_z2, r_z2, s_x1, r_x1,
     s_g, r_g, s_y1z, r_y1z) = scratch

    wide = lax.axis_index("wide")
    x = lax.axis_index("pair")
    core = wide % 2
    chip = wide // 2
    z = chip % Z
    y = chip // Z

    def at(dx=0, dy=0, dz=0, dc=0):
        row = ((y + dy) % Y) * Z + (z + dz) % Z
        return (row * 2 + (core + dc) % 2, (x + dx) % X)

    def send(src, dst, ssem, rsem, peer):
        copy = pltpu.make_async_remote_copy(
            src_ref=src, dst_ref=dst, send_sem=ssem, recv_sem=rsem, device_id=peer, device_id_type=MESH
        )
        copy.start()
        return copy

    def all_of(space, ssem, rsem):
        return pltpu.make_async_remote_copy(
            src_ref=space, dst_ref=space, send_sem=ssem, recv_sem=rsem, device_id=at(dc=1), device_id_type=MESH
        )

    far_z, far_y, far_x = farthest_first(Z), farthest_first(Y), farthest_first(X)
    zc_peers = [(dc, dz) for dz in far_z + [0] for dc in range(2) if dc or dz]
    yc_peers = [(dc, dy) for dy in far_y + [0] for dc in range(2) if dc or dy]
    xc_peers = [(dc, dx) for dx in far_x + [0] for dc in range(2) if dc or dx]

    small = [
        pltpu.make_async_copy(src, dst, small_sem.at[i])
        for i, (src, dst) in enumerate(((sketch_in, sketch), (basis_b_in, basis_bt), (basis_a_in, basis_at)))
    ]
    small[0].start()
    barrier = pltpu.get_barrier_semaphore()
    met = 0
    for dc, dz in zc_peers:
        pl.semaphore_signal(barrier, inc=1, device_id=at(dz=dz, dc=dc), device_id_type=MESH)
        met += 1
    for dc, dy in yc_peers:
        if dy:
            pl.semaphore_signal(barrier, inc=1, device_id=at(dy=dy, dc=dc), device_id_type=MESH)
            met += 1
    for dc, dx in xc_peers:
        if dx:
            pl.semaphore_signal(barrier, inc=1, device_id=at(dx=dx, dc=dc), device_id_type=MESH)
            met += 1

    for load in small[1:]:
        load.start()
    loads = [
        pltpu.make_async_copy(blocks.at[pl.ds(i * RC, RC)], block_in.at[i], in_sem.at[i]) for i in range(Y)
    ]
    for load in loads:
        load.start()

    twice = one_hot(iota((64, 128), 1) % 64 == iota((64, 128), 0))
    small[0].wait()
    s_mine = dot(sketch[...], twice)
    s_own[...] = s_mine
    zc = z * 2 + core
    s_zc[zc] = s_mine
    small[1].wait()
    basis2 = jnp.concatenate([basis_bt[...], basis_bt[...]], axis=0)

    def narrow(i, carry):
        pltpu.make_async_copy(blocks.at[pl.ds(i * RC, RC)], block_in.at[i], in_sem.at[i]).wait()
        wide_n[...] = dot(block_in[i], basis2, CONTRACT_LAST)
        low = low_half((FC, 128))
        odd = (iota((FC, 128), 1) // 32) % 2 == 1
        for t in range(2):
            part = [wide_n[pl.ds(t * 4 + q, FC, stride=8), :] for q in range(4)]
            first = jnp.where(low, part[0], part[2])
            second = jnp.where(low, part[1], part[3])
            lanes = slice(t * 128, t * 128 + 128)
            by_a[0, i, :, lanes] = jnp.where(odd, pltpu.roll(second, 32, 1), first).astype(BF16)
            by_a[1, i, :, lanes] = jnp.where(odd, second, pltpu.roll(first, 96, 1)).astype(BF16)
        return carry

    pl.semaphore_wait(barrier, met)

    for dc, dz in zc_peers:
        send(s_own, s_zc.at[zc], s_a, r_a, at(dz=dz, dc=dc))
    got_a = all_of(s_zc.at[pl.ds(1, ZC - 1)], s_a, r_a)

    lax.fori_loop(0, Y, narrow, 0)

    got_a.wait_recv()
    half = ZC // 2
    lo = jnp.concatenate([s_zc[i] for i in range(half)], axis=0)
    hi = jnp.concatenate([s_zc[half + i] for i in range(half)], axis=0)
    rows_h = half * 4
    s_y[y] = jnp.where(low_half((rows_h, 128)), lo, hi).astype(BF16)
    for dy in far_y:
        send(s_y.at[y], s_y.at[y], s_b, r_b, at(dy=dy))
    got_b = all_of(s_y.at[pl.ds(1, Y - 1)], s_b, r_b)

    partner = at(dc=1)
    small[2].wait()

    lane_in = iota((256, 256), 0)
    move = one_hot(iota((256, 256), 1) == (lane_in // 8 % 4) * 64 + lane_in // 32 * 8 + lane_in % 8)
    for cc in range(2):
        packed[cc] = dot(by_a[cc].reshape(FX, 256), move).astype(BF16).reshape(Y, FC, 256)

    ZA = Z * 16
    a_part = basis_at[:, pl.ds(pl.multiple_of(y * ZA, ZA), ZA)]
    MR = chips * 4

    def chip_of(index):
        zy = index // 4
        return (zy % Y) * Z + zy // Y

    col = iota((ZA, 256), 1)
    pick = iota((ZA, 256), 0) == (
        z * 16 + ((core + (col // 32) % 2) % 2) * 8 + ((col // 8) % 4) * 2 + (col // 64) % 2
    )
    a_cols = dot(a_part, one_hot(pick)).astype(BF16)
    spread = one_hot(chip_of(iota((MR, chips), 0)) == iota((MR, chips), 1))
    rows_a = dot(spread, a_cols)
    for rh in range(2):
        keep = iota((MR, 256), 1) % 8 == rh * 4 + iota((MR, 256), 0) % 4
        m_to[rh] = jnp.where(keep, rows_a, 0.0).astype(BF16)

    got_b.wait_recv()
    low = low_half((rows_h, 128))
    for i in range(Y):
        v = s_y[i].astype(F32)
        w = swap_halves(v)
        s_all[2 * i * rows_h : (2 * i + 1) * rows_h, :] = jnp.where(low, v, w).astype(BF16)
        s_all[(2 * i + 1) * rows_h : (2 * i + 2) * rows_h, :] = jnp.where(low, w, v).astype(BF16)

    low = low_half((8, 128))
    for cc in range(2):
        t = dot(packed[cc].reshape(FX, 256), s_all[...], CONTRACT_FIRST)
        for xx in range(4):
            for ah in range(4):
                at_a = xx * 64 + ah * 16
                t_out[cc, xx, ah] = jnp.where(low, t[at_a : at_a + 8], t[at_a + 8 : at_a + 16])
    for dc, dx in xc_peers:
        send(t_out.at[(core + dc) % 2, (x + dx) % X], t_in.at[dc * X + dx], s_t, r_t, at(dx=dx, dc=dc))
    got_t = all_of(t_in.at[pl.ds(1, 2 * X - 1)], s_t, r_t)

    def spread_fibres(peers):
        for dc, dy in peers:
            send(packed.at[(core + dc) % 2, (y + dy) % Y], n_in.at[dc * Y + dy], s_n, r_n, at(dy=dy, dc=dc))

    spread_fibres([p for p in yc_peers if p[0] == 0])
    mine = t_out[core, x]
    for copy in (got_a, got_b):
        copy.wait_send()
    got_t.wait_recv()
    for dx in range(1, X):
        mine = mine + t_in[dx]
    other = t_in[X]
    for dx in range(1, X):
        other = other + t_in[X + dx]
    u = jnp.concatenate([mine.reshape(32, 128), other.reshape(32, 128)], axis=0)
    low = low_half((64, 128))
    v = swap_halves(u)
    u = jnp.concatenate([jnp.where(low, u, v), jnp.where(low, v, u)], axis=0)
    top = u.astype(BF16)
    rest = (u - top.astype(F32)).astype(BF16)
    u = jnp.concatenate([top, rest], axis=0)
    low = low_half((MR, 128))
    part = jnp.where(low, dot(m_to[0], u), dot(m_to[1], u))
    RZ = Y * 4
    for i in range(Z):
        sp_out[i] = part[i * RZ : (i + 1) * RZ].astype(BF16)

    for dz in far_z:
        send(sp_out.at[(z + dz) % Z], sp_in.at[dz], s_z1, r_z1, at(dz=dz))
    got_z = all_of(sp_in.at[pl.ds(1, Z - 1)], s_z1, r_z1)
    total = sp_out[z].astype(F32)
    got_t.wait_send()

    row = iota((128, ZA), 0)
    pick = one_hot(iota((128, ZA), 1) == z * 16 + ((core + row // 64) % 2) * 8 + (row // 8) % 8)
    spread = one_hot(chip_of(iota((chips, MR), 1)) == iota((chips, MR), 0))
    for dy in range(Y):
        a_part = basis_at[:, pl.ds(pl.multiple_of(((y + Y - dy) % Y) * ZA, ZA), ZA)]
        cols_a = dot(dot(pick, a_part, CONTRACT_LAST).astype(BF16), spread)
        for rh in range(2):
            keep = iota((128, MR), 0) % 8 == rh * 4 + iota((128, MR), 1) % 4
            m_from[dy * 128 : dy * 128 + 128, rh * MR : (rh + 1) * MR] = jnp.where(keep, cols_a, 0.0).astype(BF16)

    got_z.wait_recv()
    for dz in range(1, Z):
        total = total + sp_in[dz].astype(F32)
    z_out[...] = total.astype(BF16)
    for dy in far_y:
        send(z_out, z_in.at[dy], s_y1, r_y1, at(dy=dy))
    got_r = all_of(z_in.at[pl.ds(1, Y - 1)], s_y1, r_y1)
    got_z.wait_send()
    got_r.wait_recv()
    for dy in range(1, Y):
        total = total + z_in[dy].astype(F32)
    for i in range(Y):
        mz[i] = total[i * 4 : i * 4 + 4]
    s_full[x, z] = total.astype(BF16)
    spot = s_full.at[x, z]
    got = {dz: send(spot, spot, s_z2, r_z2.at[dz], at(dz=dz)) for dz in far_z}
    spread_fibres([p for p in yc_peers if p[0] == 1])
    got_n = all_of(n_in.at[pl.ds(1, 2 * Y - 1)], s_n, r_n)
    got_r.wait_send()
    for dz in [0] + nearest_first(Z):
        if dz:
            got[dz].wait_recv()
        spot = s_full.at[x, (z + Z - dz) % Z]
        for dx in far_x:
            send(spot, spot, s_x1.at[dx], r_x1.at[dx], at(dx=dx))
    got_x = [all_of(s_full.at[(x + X - dx) % X], s_x1.at[dx], r_x1.at[dx]) for dx in nearest_first(X)]
    all_of(sp_in.at[pl.ds(1, Z - 1)], s_z2, r_z2.at[0]).wait_send()

    got_n.wait_recv()
    half = low_half((FC, 128))
    for dy in range(Y):
        own = (n_in[dy] if dy else packed[core, y]).astype(F32)
        other = n_in[Y + dy].astype(F32)
        spot = slice(dy * 128, dy * 128 + 128)
        for xp in range(X // 2):
            a_side = own[:, xp * 128 : xp * 128 + 128]
            b_side = other[:, xp * 128 : xp * 128 + 128]
            n_x[2 * xp, :, spot] = jnp.where(half, a_side, swap_halves(b_side)).astype(BF16)
            n_x[2 * xp + 1, :, spot] = jnp.where(half, swap_halves(a_side), b_side).astype(BF16)
    for copy in got_x:
        copy.wait_recv()
    s_x = [s_full[i].reshape(MR, 128) for i in range(X)]

    big = dot(s_x[0], s_x[0], CONTRACT_FIRST)
    for i in range(1, X):
        big = big + dot(s_x[i], s_x[i], CONTRACT_FIRST)
    gram_out[...] = swap_halves(big[0:64]) + big[64:128]
    got_g = send(gram_out, gram_in, s_g, r_g, partner)

    low = low_half((MR, 128))
    rhs = []
    for xp in range(X // 2):
        s0 = s_x[2 * xp].astype(F32)
        s1 = s_x[2 * xp + 1].astype(F32)
        rhs.append(
            jnp.concatenate(
                [jnp.where(low, s0, swap_halves(s1)), jnp.where(low, swap_halves(s0), s1)], axis=0
            ).astype(BF16)
        )
    w_rows = dot(m_from[...], jnp.concatenate(rhs, axis=1)).astype(BF16)
    by_x = dot(n_x[...].reshape(X * FC, Y * 128), w_rows)
    even = by_x[0:FC, 0:128]
    odd = by_x[FC : 2 * FC, 0:128]
    for xp in range(1, X // 2):
        even = even + by_x[2 * xp * FC : (2 * xp + 1) * FC, xp * 128 : xp * 128 + 128]
        odd = odd + by_x[(2 * xp + 1) * FC : (2 * xp + 2) * FC, xp * 128 : xp * 128 + 128]
    ypart = jnp.where(half, even + swap_halves(odd), swap_halves(even) + odd)
    ypart = jnp.where(low_half((FC // 2, 128)), ypart[0 : FC // 2], ypart[FC // 2 : FC])
    for i in range(ZL):
        for cc in range(2):
            y_out[i, cc] = ypart[i * 8 + cc * 4 : i * 8 + cc * 4 + 4]
    for dc, dz in zc_peers:
        send(y_out.at[((z + dz) % Z) % ZL, (core + dc) % 2], y_in.at[dc * Z + dz], s_y1z, r_y1z, at(dz=dz, dc=dc))
    got_y = all_of(y_in.at[pl.ds(1, 2 * Z - 1)], s_y1z, r_y1z)

    got_g.wait_recv()
    g = gram_out[...] + gram_in[...]
    low = low_half((64, 128))
    g = jnp.where(low, jnp.where(iota((64, 128), 0) == iota((64, 128), 1), 1.0, 0.0), g)
    tiles = [g[i * 8 : i * 8 + 8] for i in range(8)]
    sub = iota((8, 128), 0)

    def lane(v, j):
        return jnp.broadcast_to(v[:, 64 + j : 65 + j], v.shape)

    def eliminate(tiles, first, last):
        for j in range(first, last, 4):
            home, pos = j // 8, j % 8
            lines = [tiles[home][pos + t : pos + t + 1] for t in range(4)]
            u = [[lane(lines[t], j + v) for v in range(4)] for t in range(4)]
            inv = []
            for t in range(4):
                inv.append(1.0 / u[t][t])
                for v in range(t + 1, 4):
                    ratio = u[t][v] * inv[t]
                    for w in range(v, 4):
                        u[v][w] = u[v][w] - ratio * u[t][w]
                    lines[v] = lines[v] - ratio * lines[t]
            for i in range(home, 8):
                c = [lane(tiles[i], j + v) for v in range(4)]
                new = tiles[i]
                for t in range(4):
                    m = c[t] * inv[t]
                    if i == home:
                        m = jnp.where(sub > pos + t, m, 0.0)
                    for v in range(t + 1, 4):
                        c[v] = c[v] - m * u[t][v]
                    new = new - m * lines[t]
                tiles[i] = new
        return tiles

    tiles = eliminate(tiles, 0, 64)
    elim = jnp.concatenate(tiles, axis=0)
    diagonal = jnp.where(iota((64, 128), 1) == iota((64, 128), 0) + 64, elim, 0.0)
    pivots = jnp.sum(diagonal, axis=1, keepdims=True)
    inverse = elim * (1.0 / jnp.sqrt(pivots))

    for copy in (got_n, *got_x, got_g, got_y):
        copy.wait_send()
    acc = y_out[z % ZL, core]
    got_y.wait_recv()
    for i in range(1, 2 * Z):
        acc = acc + y_in[i]
    acc = jnp.where(z // ZL == 0, acc, swap_halves(acc))
    s_mine = mz[y]
    rows = jnp.concatenate([s_mine, swap_halves(s_mine), acc, acc], axis=0)
    out = dot(rows[:, 0:64], inverse[:, 0:64], CONTRACT_LAST, lax.Precision.HIGHEST)
    rows_out[0:8, 0:64] = out[0:8] * float((chips * 64) ** 0.5)
    rows_out[8:16, 0:64] = out[8:16]


def scratch_for(sizes, cb):
    X, Y, Z = sizes
    ZC = Z * 2
    ZL = Z // 2
    chips = Y * Z
    FX = chips * 8
    FC = FX // Y
    MR = chips * 4
    RZ = Y * 4
    dma = pltpu.SemaphoreType.DMA
    return [
        pltpu.VMEM((Y, FC * 8, cb), BF16),
        pltpu.VMEM((FC * 8, 128), F32),
        pltpu.VMEM((2, Y, FC, 256), BF16),
        pltpu.VMEM((2, Y, FC, 256), BF16),
        pltpu.VMEM((2 * Y, FC, 256), BF16),
        pltpu.VMEM((X, FC, Y * 128), BF16),
        pltpu.VMEM((4, 128), F32),
        pltpu.VMEM((ZC, 4, 128), F32),
        pltpu.VMEM((Y, ZC * 2, 128), BF16),
        pltpu.VMEM((FX, 128), BF16),
        pltpu.VMEM((2, 4, 4, 8, 128), F32),
        pltpu.VMEM((2 * X, 4, 8, 128), F32),
        pltpu.VMEM((Z, RZ, 128), BF16),
        pltpu.VMEM((Z, RZ, 128), BF16),
        pltpu.VMEM((RZ, 128), BF16),
        pltpu.VMEM((Y, RZ, 128), BF16),
        pltpu.VMEM((Y, 4, 128), F32),
        pltpu.VMEM((X, Z, RZ, 128), BF16),
        pltpu.VMEM((2, MR, 256), BF16),
        pltpu.VMEM((Y * 128, 2 * MR), BF16),
        pltpu.VMEM((64, 128), F32),
        pltpu.VMEM((64, 128), F32),
        pltpu.VMEM((ZL, 2, 4, 128), F32),
        pltpu.VMEM((2 * Z, 4, 128), F32),
        pltpu.VMEM((64, cb), BF16),
        pltpu.VMEM((chips, chips * 16), BF16),
        pltpu.VMEM((4, 64), BF16),
        dma((Y,)),
        dma((3,)),
        dma, dma,
        dma, dma,
        dma, dma,
        dma, dma,
        dma, dma,
        dma, dma,
        dma, dma((Z,)),
        dma((X,)), dma((X,)),
        dma, dma,
        dma, dma,
    ]


def per_device(sizes, blocks, basis_a, basis_b, sketch):
    fibres, own_a, cb = blocks.shape
    vmem = pl.BlockSpec(memory_space=pltpu.VMEM)
    anywhere = pl.BlockSpec(memory_space=pl.ANY)
    rows = pl.pallas_call(
        functools.partial(kernel, sizes),
        out_shape=jax.ShapeDtypeStruct((16, 128), F32),
        in_specs=[anywhere] * 4,
        out_specs=vmem,
        scratch_shapes=scratch_for(sizes, cb),
        compiler_params=pltpu.CompilerParams(collective_id=0, has_side_effects=True),
        name="tucker",
    )(blocks.reshape(fibres * own_a, cb), basis_b.T, basis_a.T, sketch)
    return pl.pallas_call(
        finish,
        out_shape=(jax.ShapeDtypeStruct((8, 64), F32), jax.ShapeDtypeStruct((4, 64), F32)),
        in_specs=[vmem],
        out_specs=(vmem, vmem),
        name="finish",
    )(rows)


def solution(mesh):
    chips = mesh.shape["wide"] // 2
    side = int(round(chips ** 0.5))
    sizes = (mesh.shape["pair"], side, chips // side)
    placed = (P("pair", "wide", None), P(), P(), P(("pair", "wide"), None))
    return jax.shard_map(
        functools.partial(per_device, sizes),
        mesh=mesh,
        in_specs=placed,
        out_specs=(P(("wide", "pair"), None), P(("pair", "wide"), None)),
        check_vma=False,
    )
```
